32 devices in a mesh: seq: 8 (over y, x, core), head: 4 (over z).
Axes of the slice: x: 2, y: 2, z: 4, core: 2. Of those that a mesh axis runs over, the one named last changes fastest.
Arguments:
- query: bfloat16 [1024, 96, 128], P(('seq', 'head')), may hold values from -15.6 to 15.6
- key_new: bfloat16 [1024, 8, 128], P('seq', 'head'), may hold values from -6 to 6
- value_new: bfloat16 [1024, 8, 128], P('seq', 'head'), may hold values from -6 to 6
- key_old: bfloat16 [1024, 8, 128], P('seq', 'head'), may hold values from -6 to 6
- value_old: bfloat16 [1024, 8, 128], P('seq', 'head'), may hold values from -6 to 6
- offset: int32 [1], replicated, may hold values from 0 to 1023
- windows: int32 [8], P('head'), may hold values from 512 to 1024, as said below
- grad_out: bfloat16 [1024, 96, 128], P(('seq', 'head')), may hold values from -6 to 6
Outputs:
- grad_query: float32 [1024, 96, 128], P(('seq', 'head'))
- grad_key_new: float32 [1024, 8, 128], P('seq', 'head')
- grad_value_new: float32 [1024, 8, 128], P('seq', 'head')
- grad_key_old: float32 [1024, 8, 128], P('seq', 'head')
- grad_value_old: float32 [1024, 8, 128], P('seq', 'head')
The draws below stay inside these ranges and needn't reach their ends.
Inputs may be any that keep to these rules, and one draw needn't show every extreme that they name: `windows`: one key-value head has a window of exactly 1024 tokens and another of exactly 512.
All inputs are finite; a program needn't handle non-finite values.
Results may differ from the reference program's by a relative error of at most 0.003.
Values may be sent and summed in bfloat16 or wider, within the bound.
A program may use at most 128 MiB of HBM per device.

```python
import math
import jax
import jax.numpy as jnp
from jax import lax

HQ = 96
KVH = 8
HD = 128
GROUP = 12
STRETCH = 1024


def draw_query(key, part):
    values = jax.random.truncated_normal(jax.random.fold_in(key, 23), -6.0, 6.0, (STRETCH, HQ, HD), jnp.float32)
    return values.astype(jnp.bfloat16)


def draw_key_new(key, part):
    values = jax.random.truncated_normal(jax.random.fold_in(key, 33), -6.0, 6.0, (STRETCH, KVH, HD), jnp.float32)
    return values.astype(jnp.bfloat16)


def draw_windows(key, part):
    picks = jax.random.randint(jax.random.fold_in(key, 41), (KVH,), STRETCH // 2, STRETCH + 1)
    order = jax.random.permutation(jax.random.fold_in(key, 42), KVH)
    places = jnp.arange(KVH)
    picks = jnp.where(places == order[0], STRETCH, picks)
    picks = jnp.where(places == order[1], STRETCH // 2, picks)
    return picks.astype(jnp.int32)


def shard_levels(rng, dims, split, least, top_value):
    gain, own = 1.0, jax.random.fold_in(rng, 6)
    for position, shards_of in split:
        heights = jnp.exp(jax.random.uniform(jax.random.fold_in(own, position), (shards_of,), jnp.float32, least / len(split), top_value / len(split)))
        gain = gain * jnp.repeat(heights, dims[position] // shards_of).reshape([-1 if axis == position else 1 for axis in range(len(dims))])
    return gain


def normal_values(key, extent, scale, most, pieces=(), held_as=jnp.bfloat16):
    values = jax.random.normal(key, extent, jnp.float32) * scale
    if len(pieces) > 0:
        values = shard_levels(key, extent, pieces, -0.22, 0.18) * values
    return jnp.clip(values, min=-most, max=most).astype(held_as)


def setup_inputs(seed: int = 0) -> dict:
    key_of = jax.random.split(jax.random.key(seed), 9)
    query = draw_query(jax.random.fold_in(key_of[8], 71), 0)
    key_new = draw_key_new(jax.random.fold_in(key_of[8], 71), 0)
    value_new = normal_values(key_of[2], (STRETCH, KVH, HD), 1.0, 6.0, ((0, 8), (1, 4)))
    key_old = normal_values(key_of[3], (STRETCH, KVH, HD), 1.0, 6.0, ((0, 8), (1, 4)))
    value_old = normal_values(key_of[4], (STRETCH, KVH, HD), 1.0, 6.0, ((0, 8), (1, 4)))
    offset = jax.random.randint(key_of[5], (1,), 0, STRETCH).astype(jnp.int32)
    windows = draw_windows(jax.random.fold_in(key_of[8], 71), 0)
    grad_out = normal_values(key_of[7], (STRETCH, HQ, HD), 1.0, 6.0, ((0, 32),))
    return {"query": query, "key_new": key_new, "value_new": value_new, "key_old": key_old, "value_old": value_old, "offset": offset, "windows": windows, "grad_out": grad_out}


def reference(query, key_new, value_new, key_old, value_old, offset, windows, grad_out):
    score_scale = 1.0 / math.sqrt(HD)
    slot_order = (jnp.arange(STRETCH, dtype=jnp.int32) + offset[0]) % STRETCH
    all_keys = jnp.concatenate([key_old[slot_order], key_new], axis=0)
    all_values = jnp.concatenate([value_old[slot_order], value_new], axis=0)
    row_block = math.gcd(STRETCH, 128)
    key_span = STRETCH + row_block
    block_starts = jnp.arange(STRETCH // row_block, dtype=jnp.int32) * row_block

    def visit_block(state_in, row_start):
        key_grads, value_grads = state_in
        queries = lax.dynamic_slice_in_dim(query, row_start, row_block, 0).astype(jnp.float32).reshape(row_block, KVH, GROUP, HD)
        out_grads = lax.dynamic_slice_in_dim(grad_out, row_start, row_block, 0).astype(jnp.float32).reshape(row_block, KVH, GROUP, HD)
        key_rows = lax.dynamic_slice_in_dim(all_keys, row_start, key_span, 0).astype(jnp.float32)
        value_rows = lax.dynamic_slice_in_dim(all_values, row_start, key_span, 0).astype(jnp.float32)
        query_pos = row_start + jnp.arange(row_block, dtype=jnp.int32)
        key_pos = row_start + jnp.arange(key_span, dtype=jnp.int32) - STRETCH
        key_row = key_pos[None, None, None, :]
        query_col = query_pos[:, None, None, None]
        seen = (key_row <= query_col) & (key_row > query_col - windows[None, :, None, None])
        scores = score_scale * jnp.einsum('qgjd,kgd->qgjk', queries, key_rows)
        masked = jnp.where(seen, scores, -jnp.inf)
        row_top = lax.optimization_barrier(jnp.max(masked, axis=-1, keepdims=True))
        log_total = row_top + jnp.log(lax.optimization_barrier(jnp.sum(jnp.exp(masked - row_top), axis=-1, keepdims=True)))
        weights = jnp.where(seen, jnp.exp(scores - log_total), 0.0)
        weight_grad = jnp.einsum('qgjd,kgd->qgjk', out_grads, value_rows)
        row_delta = lax.optimization_barrier(jnp.sum(weights * weight_grad, axis=-1, keepdims=True))
        dscore = lax.optimization_barrier((weights * (weight_grad - row_delta)).astype(jnp.bfloat16)).astype(jnp.float32)
        weights_low = lax.optimization_barrier(weights.astype(jnp.bfloat16)).astype(jnp.float32)
        query_grad = score_scale * jnp.einsum('qgjk,kgd->qgjd', dscore, key_rows)
        key_part = score_scale * jnp.einsum('qgjk,qgjd->kgd', dscore, queries)
        value_part = jnp.einsum('qgjk,qgjd->kgd', weights_low, out_grads)
        key_grads = lax.dynamic_update_slice_in_dim(key_grads, lax.dynamic_slice_in_dim(key_grads, row_start, key_span, 0) + key_part, row_start, 0)
        value_grads = lax.dynamic_update_slice_in_dim(value_grads, lax.dynamic_slice_in_dim(value_grads, row_start, key_span, 0) + value_part, row_start, 0)
        return ((key_grads, value_grads), query_grad.reshape(row_block, HQ, HD))
    zero_grads = jnp.zeros((2 * STRETCH, KVH, HD), jnp.float32)
    final_state, query_blocks = lax.scan(visit_block, (zero_grads, zero_grads), block_starts)
    key_grads, value_grads = final_state
    grad_query = query_blocks.reshape(STRETCH, HQ, HD)
    back_order = (jnp.arange(STRETCH, dtype=jnp.int32) - offset[0]) % STRETCH
    return (grad_query, key_grads[STRETCH:], value_grads[STRETCH:], key_grads[:STRETCH][back_order], value_grads[:STRETCH][back_order])
```

```python
import functools
import math

import jax
import jax.numpy as jnp
from jax import lax
from jax.experimental import pallas as pl
from jax.experimental.pallas import tpu as pltpu
from jax.sharding import PartitionSpec as P

MESH = pl.DeviceIdType.MESH
NT = (((1,), (1,)), ((), ()))
NN = (((1,), (0,)), ((), ()))


def dot(a, b, dims):
    return lax.dot_general(a, b, dims, preferred_element_type=jnp.float32)


def kernel(
    heads, seqs, per_group, heads_at_once,
    win_ref, off_ref, q_ref, do_ref, kv_ref,
    dq_ref, grad_ref,
    wide, q_mine, do_mine, q_all, do_all, kv_all, line, keys_t, bias, sums,
    term_out, term_in, fold_in, fold_out, dq_out, dq_in,
    q_send, q_recv, do_send, do_recv, dq_send, dq_recv,
    win_out, win_in, win_sems, kv_send, far_send, pass_send, kv_recv, term_send, fold_send, far_back_send, term_recv, fold_recv,
):
    hb = heads_at_once
    half = heads // 2
    chips = seqs // 2
    me_h, me_s = lax.axis_index("head"), lax.axis_index("seq")
    chip, side = me_s // 2, lax.rem(me_s, 2)
    pair, place = me_h // half, lax.rem(me_h, half)
    rows, all_heads, width = q_ref.shape
    mine = all_heads // heads
    groups = mine // per_group
    tokens = rows * heads
    run = rows * half
    total = tokens * seqs
    span = total + tokens + run
    steps = per_group // hb
    chunks = groups * steps
    scale = 1.0 / math.sqrt(width)
    even, odd = side == 0, side == 1
    far_h = lax.rem(me_h + half, heads)
    my_order = side * half + place
    first_token = chip * 2 * tokens + pair * run

    def set_of(seq_side, head):
        return lax.rem(head + seq_side * half, heads)

    peers = []
    for di in range(2):
        for dj in range(half):
            if di + dj == 0:
                continue
            there_side = lax.rem(side + di, 2)
            there_place = lax.rem(place + dj, half)
            there_h = pair * half + there_place
            peers.append((chip * 2 + there_side, there_h, there_side * half + there_place, set_of(there_side, there_h)))

    def row_copy(src, dst, send, recv, chunk, peer, from_slot, to_slot, order):
        part = pl.ds(chunk * hb, hb)
        return pltpu.make_async_remote_copy(
            src_ref=src.at[from_slot, part], dst_ref=dst.at[to_slot, part],
            send_sem=send.at[chunk, peer[2]], recv_sem=recv.at[chunk, order],
            device_id={"seq": peer[0], "head": peer[1]}, device_id_type=MESH,
        )

    def q_copies(chunk, peer, order):
        return (
            row_copy(q_mine, q_all, q_send, q_recv, chunk, peer, peer[3], my_order, order),
            row_copy(do_mine, do_all, do_send, do_recv, chunk, peer, peer[3], my_order, order),
        )

    def dq_copy(chunk, peer, order):
        return row_copy(dq_out, dq_in, dq_send, dq_recv, chunk, peer, peer[2], my_order, order)

    def chip_at(k):
        return lax.rem(chip + k, chips)

    def kv_copy(group, there_chip, owner):
        return pltpu.make_async_remote_copy(
            src_ref=kv_ref.at[group], dst_ref=kv_all.at[group, owner],
            send_sem=kv_send.at[group, there_chip], recv_sem=kv_recv.at[group, owner],
            device_id={"seq": there_chip * 2, "head": me_h}, device_id_type=MESH,
        )

    def far_copy(group, owner):
        return pltpu.make_async_remote_copy(
            src_ref=kv_ref.at[group], dst_ref=kv_all.at[group, owner],
            send_sem=far_send.at[group], recv_sem=kv_recv.at[group, owner],
            device_id={"seq": chip * 2 + 1, "head": far_h}, device_id_type=MESH,
        )

    def pass_copy(group, k, there_chip):
        owner = chip * 2 + k
        return pltpu.make_async_remote_copy(
            src_ref=kv_all.at[group, owner], dst_ref=kv_all.at[group, owner],
            send_sem=pass_send.at[group, k, there_chip], recv_sem=kv_recv.at[group, owner],
            device_id={"seq": there_chip * 2 + 1, "head": me_h}, device_id_type=MESH,
        )

    def term_copy(group, kind, there, slot):
        return pltpu.make_async_remote_copy(
            src_ref=term_out.at[group, kind, there], dst_ref=term_in.at[group, kind, slot],
            send_sem=term_send.at[group, kind, there], recv_sem=term_recv.at[group, kind, slot],
            device_id={"seq": there, "head": me_h}, device_id_type=MESH,
        )

    def fold_copy(group, kind, there_chip, slot):
        return pltpu.make_async_remote_copy(
            src_ref=term_out.at[group, kind, pl.ds(there_chip * 2, 2)], dst_ref=fold_in.at[group, kind, slot],
            send_sem=fold_send.at[group, kind, there_chip], recv_sem=fold_recv.at[group, kind, slot],
            device_id={"seq": there_chip * 2 + 1, "head": me_h}, device_id_type=MESH,
        )

    def far_back_copy(group, kind, k):
        return pltpu.make_async_remote_copy(
            src_ref=fold_out.at[group, kind, k], dst_ref=term_in.at[group, kind, chips],
            send_sem=far_back_send.at[group, kind, k], recv_sem=term_recv.at[group, kind, chips],
            device_id={"seq": chip * 2 + k, "head": far_h}, device_id_type=MESH,
        )

    def win_copy():
        return pltpu.make_async_remote_copy(
            src_ref=win_out, dst_ref=win_in, send_sem=win_sems.at[0], recv_sem=win_sems.at[1],
            device_id={"head": far_h}, device_id_type=MESH,
        )

    barrier = pltpu.get_barrier_semaphore()
    other = chip * 2 + 1 - side
    for k in range(1, heads):
        for seq in (me_s, other):
            pl.semaphore_signal(
                barrier, inc=1, device_id={"seq": seq, "head": lax.rem(me_h + k, heads)}, device_id_type=MESH
            )
    for k in range(1, seqs):
        pl.semaphore_signal(barrier, inc=1, device_id={"seq": lax.rem(me_s + k, seqs), "head": me_h}, device_id_type=MESH)

    for ref, out in ((q_ref, q_mine), (do_ref, do_mine)):
        wide[...] = ref[...].astype(jnp.float32).reshape(rows * all_heads, width)
        for head in range(all_heads):
            out[head // mine, head % mine] = wide[pl.ds(head, rows, stride=all_heads)].astype(jnp.bfloat16)

    for group in range(groups):
        win_out[group] = jnp.full(win_out.shape[1:], win_ref[group], jnp.int32)

    pl.semaphore_wait(barrier, 2 * (heads - 1) + seqs - 1)

    @pl.when(odd)
    def _():
        win_copy().start()

    for group in range(groups):
        far_copy(group, me_s).start()

        @pl.loop(1, chips)
        def _(k):
            kv_copy(group, chip_at(k), me_s).start()

        @pl.when(odd)
        def _():
            kv_copy(group, chip, me_s).start()

    @pl.loop(0, chunks)
    def _(chunk):
        for peer in peers:
            for copy in q_copies(chunk, peer, my_order):
                copy.start()

    my_set = set_of(side, me_h)
    q_all[my_order] = q_mine[my_set]
    do_all[my_order] = do_mine[my_set]

    @pl.when(even)
    def _():
        win_in[...] = win_out[...]
        for group in range(groups):
            kv_all[group, me_s] = kv_ref[group]

    @pl.when(odd)
    def _():
        for group in range(groups):
            for k in range(2):
                far_copy(group, chip * 2 + k).wait_recv()

                @pl.loop(1, chips)
                def _(step):
                    pass_copy(group, k, chip_at(step)).start()

        win_copy().wait_recv()

    old_rows = pl.multiple_of(total - first_token, run)
    base = lax.rem(off_ref[0] + first_token, total)

    for group in range(groups):
        @pl.loop(0, seqs)
        def _(owner):
            @pl.when((even & (owner != me_s)) | (odd & (owner // 2 != chip)))
            def _():
                far_copy(group, owner).wait_recv()

        for kind in range(2):
            @pl.loop(0, seqs)
            def _(owner):
                sums[kind, pl.ds(owner * tokens, tokens)] = kv_all[group, owner, kind].astype(jnp.float32)

            sums[kind, total : total + tokens] = sums[kind, :tokens]

            @pl.loop(0, (old_rows + tokens - 1) // tokens)
            def _(block):
                start = lax.rem(base + block * tokens, total)
                line[kind, pl.ds(pl.multiple_of(block * tokens, tokens), tokens)] = sums[
                    kind, pl.ds(start, tokens)
                ].astype(jnp.bfloat16)

            @pl.loop(0, 2 * chip + 2)
            def _(block):
                line[kind, pl.ds(pl.multiple_of(old_rows + block * tokens, run), tokens)] = kv_all[group, block, 2 + kind]

        window = win_in[group, :1]
        position = lax.broadcasted_iota(jnp.int32, (span, tokens), 0) - total
        column = lax.broadcasted_iota(jnp.int32, (span, tokens), 1)
        token = jnp.where(column >= run, column + (tokens - run), column)
        bias[...] = jnp.where((position <= token) & (position > token - window), 0.0, -jnp.inf)
        keys_t[...] = line[0, :span].T
        sums[...] = jnp.zeros_like(sums)

        @pl.loop(0, steps)
        def _(step):
            chunk = group * steps + step
            first = chunk * hb
            for peer in peers:
                for copy in q_copies(chunk, peer, peer[2]):
                    copy.wait_recv()
            q = jnp.concatenate([q_all[:, first + h].reshape(tokens, width) for h in range(hb)], 0)
            do = jnp.concatenate([do_all[:, first + h].reshape(tokens, width) for h in range(hb)], 0)
            scores = dot(line[0, :span], q, NT) + jnp.concatenate([bias[...]] * hb, 1)
            top = jnp.max(scores, axis=0, keepdims=True)
            grown = jnp.exp2((scores - top) * (scale * math.log2(math.e)))
            inverse = 1.0 / jnp.sum(grown, axis=0, keepdims=True)
            weight_grad = dot(line[1, :span], do, NT)
            delta = jnp.sum(grown * weight_grad, axis=0, keepdims=True) * inverse
            weights = grown * inverse
            dscore = (weights * (weight_grad - delta)).astype(jnp.bfloat16)
            dqt = dot(keys_t[...], dscore, NN) * scale
            for h in range(hb):
                piece = dqt[:, h * tokens : (h + 1) * tokens].T.astype(jnp.bfloat16)
                dq_out[:, first + h] = piece.reshape(heads, rows, width)
            for peer in peers:
                dq_copy(chunk, peer, my_order).start()
            sums[0, :span] += dot(dscore, q, NN)
            sums[1, :span] += dot(weights.astype(jnp.bfloat16), do, NN)

        @pl.loop(0, 2 * chip + 2)
        def _(block):
            part = pl.ds(pl.multiple_of(old_rows + block * tokens, run), tokens)
            term_out[group, 1, block, :, :width] = (sums[0, part] * scale).astype(jnp.bfloat16)
            term_out[group, 1, block, :, width:] = sums[1, part].astype(jnp.bfloat16)

        @pl.loop(old_rows // run, total // run)
        def _(block):
            for kind in range(2):
                sums[kind, pl.ds(pl.multiple_of(block * run, run), run)] = jnp.zeros((run, width), jnp.float32)

        for kind in range(2):
            sums[kind, total : total + tokens] = sums[kind, :tokens]

        @pl.loop(0, seqs)
        def _(block):
            start = lax.rem(block * tokens + total - base, total)
            term_out[group, 0, block, :, :width] = (sums[0, pl.ds(start, tokens)] * scale).astype(jnp.bfloat16)
            term_out[group, 0, block, :, width:] = sums[1, pl.ds(start, tokens)].astype(jnp.bfloat16)

        @pl.when(even)
        def _():
            @pl.loop(1, seqs)
            def _(k):
                there = lax.rem(me_s + k, seqs)
                term_copy(group, 0, there, chip).start()

                @pl.when(there // 2 <= chip)
                def _():
                    term_copy(group, 1, there, chip).start()

        @pl.when(odd)
        def _():
            @pl.loop(1, chips)
            def _(k):
                there = chip_at(k)
                fold_copy(group, 0, there, chip).start()

                @pl.when(there < chip)
                def _():
                    fold_copy(group, 1, there, chip).start()

    @pl.when(odd)
    def _():
        for group in range(groups):
            for kind in range(2):
                part = term_out.at[group, kind, pl.ds(chip * 2, 2)]
                acc = fold_in.at[group, kind, chip]
                sums[:, : tokens] = part[:, :, :width].astype(jnp.float32)
                sums[:, tokens : 2 * tokens] = part[:, :, width:].astype(jnp.float32)

                @pl.loop(1, chips)
                def _(k):
                    there = chip_at(k)

                    @pl.when((kind == 0) | (there > chip))
                    def _():
                        fold_copy(group, kind, there, there).wait_recv()
                        got = fold_in[group, kind, there].astype(jnp.float32)
                        sums[:, :tokens] += got[:, :, :width]
                        sums[:, tokens : 2 * tokens] += got[:, :, width:]

                for k in range(2):
                    fold_out[group, kind, k, :, :width] = sums[k, :tokens].astype(jnp.bfloat16)
                    fold_out[group, kind, k, :, width:] = sums[k, tokens : 2 * tokens].astype(jnp.bfloat16)
                    far_back_copy(group, kind, k).start()

    dq_ref[pl.ds(my_set * mine, mine)] = dq_out[my_order]
    for peer in peers:
        @pl.loop(0, chunks)
        def _(chunk):
            dq_copy(chunk, peer, peer[2]).wait_recv()

        dq_ref[pl.ds(peer[3] * mine, mine)] = dq_in[peer[2]]

    for group in range(groups):
        for kind in range(2):
            @pl.when(even)
            def _():
                own = term_out[group, kind, me_s].astype(jnp.float32)
                sums[0, :tokens] = own[:, :width]
                sums[1, :tokens] = own[:, width:]

            @pl.when(odd)
            def _():
                sums[:, :tokens] = jnp.zeros((2, tokens, width), jnp.float32)

            @pl.loop(0, chips + 1)
            def _(there):
                wanted = (there == chips) | (kind == 0) | (there >= chip)

                @pl.when(wanted & (odd | (there != chip)))
                def _():
                    term_copy(group, kind, me_s, there).wait_recv()
                    got = term_in[group, kind, there].astype(jnp.float32)
                    sums[0, :tokens] += got[:, :width]
                    sums[1, :tokens] += got[:, width:]

            for part in range(2):
                grad_ref[kind * 2 + part, pl.ds(group, tokens, stride=groups)] = sums[part, :tokens]

    @pl.when(odd)
    def _():
        win_copy().wait_send()

    for group in range(groups):
        far_copy(group, me_s).wait_send()

        @pl.loop(1, chips)
        def _(k):
            kv_copy(group, chip_at(k), me_s).wait_send()

        @pl.when(odd)
        def _():
            kv_copy(group, chip, me_s).wait_send()

            @pl.loop(1, chips)
            def _(step):
                there = chip_at(step)
                for k in range(2):
                    pass_copy(group, k, there).wait_send()
                fold_copy(group, 0, there, chip).wait_send()

                @pl.when(there < chip)
                def _():
                    fold_copy(group, 1, there, chip).wait_send()

            for kind in range(2):
                for k in range(2):
                    far_back_copy(group, kind, k).wait_send()

        @pl.when(even)
        def _():
            @pl.loop(1, seqs)
            def _(k):
                there = lax.rem(me_s + k, seqs)
                term_copy(group, 0, there, chip).wait_send()

                @pl.when(there // 2 <= chip)
                def _():
                    term_copy(group, 1, there, chip).wait_send()

    @pl.loop(0, chunks)
    def _(chunk):
        for peer in peers:
            for copy in q_copies(chunk, peer, my_order):
                copy.wait_send()
            dq_copy(chunk, peer, my_order).wait_send()


def shards(query, key_new, value_new, key_old, value_old, offset, windows, grad_out):
    heads, seqs = lax.axis_size("head"), lax.axis_size("seq")
    rows, all_heads, width = query.shape
    tokens = rows * heads
    total = tokens * seqs
    groups = key_new.shape[1]
    chips = seqs // 2
    run = tokens // 2
    span = total + tokens + run
    padded = total + 2 * tokens
    mine = all_heads // heads
    per_group = mine // groups
    hb = max(h for h in (1, 2, 3, 4, 6) if per_group % h == 0 and (h <= 1 or h * tokens * span <= 950_000))
    chunks = mine // hb

    kv = jnp.stack([key_old, value_old, key_new, value_new]).transpose(2, 0, 1, 3)
    vmem = pl.BlockSpec(memory_space=pltpu.VMEM)
    smem = pl.BlockSpec(memory_space=pltpu.SMEM)
    narrow, wide = jnp.bfloat16, jnp.float32
    row_shape = (heads, mine, rows, width)
    dma = pltpu.SemaphoreType.DMA
    row_sems = dma((chunks, heads))
    dq, grads = pl.pallas_call(
        functools.partial(kernel, heads, seqs, per_group, hb),
        in_specs=[smem, smem] + [vmem] * 3,
        out_specs=[vmem, vmem],
        out_shape=[
            jax.ShapeDtypeStruct((all_heads, rows, width), narrow),
            jax.ShapeDtypeStruct((4, tokens * groups, width), wide),
        ],
        scratch_shapes=[
            pltpu.VMEM((rows * all_heads, width), wide),
            pltpu.VMEM(row_shape, narrow),
            pltpu.VMEM(row_shape, narrow),
            pltpu.VMEM(row_shape, narrow),
            pltpu.VMEM(row_shape, narrow),
            pltpu.VMEM((groups, seqs, 4, tokens, width), narrow),
            pltpu.VMEM((2, padded, width), narrow),
            pltpu.VMEM((width, span), narrow),
            pltpu.VMEM((span, tokens), wide),
            pltpu.VMEM((2, padded, width), wide),
            pltpu.VMEM((groups, 2, seqs, tokens, 2 * width), narrow),
            pltpu.VMEM((groups, 2, chips + 1, tokens, 2 * width), narrow),
            pltpu.VMEM((groups, 2, chips, 2, tokens, 2 * width), narrow),
            pltpu.VMEM((groups, 2, 2, tokens, 2 * width), narrow),
            pltpu.VMEM(row_shape, narrow),
            pltpu.VMEM(row_shape, narrow),
            row_sems, row_sems, row_sems, row_sems, row_sems, row_sems,
            pltpu.VMEM((groups, 8, tokens), jnp.int32),
            pltpu.VMEM((groups, 8, tokens), jnp.int32),
            dma((2,)), dma((groups, chips)), dma((groups,)), dma((groups, 2, chips)), dma((groups, seqs)),
            dma((groups, 2, seqs)), dma((groups, 2, chips)), dma((groups, 2, 2)),
            dma((groups, 2, chips + 1)), dma((groups, 2, chips)),
        ],
        compiler_params=pltpu.CompilerParams(
            collective_id=0, has_side_effects=True, vmem_limit_bytes=62 * 2**20
        ),
    )(windows, offset, query, grad_out, kv)
    grad_query = lax.optimization_barrier(dq.transpose(1, 0, 2)).astype(wide)
    grads = grads.reshape(4, tokens, groups, width)
    return (grad_query, grads[2], grads[3], grads[0], grads[1])


def solution(mesh):
    tokens = P(("seq", "head"), None, None)
    slots = P("seq", "head", None)
    return jax.shard_map(
        shards,
        mesh=mesh,
        in_specs=(tokens, slots, slots, slots, slots, P(), P("head"), tokens),
        out_specs=(tokens, slots, slots, slots, slots),
        check_vma=False,
    )
```

```python
import functools
import math

import jax
import jax.numpy as jnp
from jax import lax
from jax.experimental import pallas as pl
from jax.experimental.pallas import tpu as pltpu
from jax.sharding import PartitionSpec as P

MESH = pl.DeviceIdType.MESH
NT = (((1,), (1,)), ((), ()))
NN = (((1,), (0,)), ((), ()))


def dot(a, b, dims):
    return lax.dot_general(a, b, dims, preferred_element_type=jnp.float32)


def plain_kernel(
    heads, seqs, per_group, heads_at_once,
    win_ref, off_ref, q_ref, do_ref, ko_ref, vo_ref, kn_ref, vn_ref,
    dq_ref, grad_ref,
    q_all, do_all, kv_all, line, keys_t, bias, sums, terms, term_out, term_in, dq_out, dq_in,
    q_send, q_recv, do_send, do_recv, kv_send, kv_recv, pass_send, dq_send, dq_recv, old_send, old_recv, new_send, new_recv,
):
    hb = heads_at_once
    me_h, me_s = lax.axis_index("head"), lax.axis_index("seq")
    rows, width = q_ref.shape[2:]
    tokens = rows * heads
    groups = q_ref.shape[1] // per_group
    total = tokens * seqs
    span = total + tokens
    steps = per_group // hb
    chunks = groups * steps
    scale = 1.0 / math.sqrt(width)

    def peer_h(k):
        return lax.rem(me_h + k, heads)

    def peer_s(k):
        return lax.rem(me_s + k, seqs)

    def row_copy(src, dst, send, recv, chunk, there, slot):
        part = pl.ds(chunk * hb, hb)
        return pltpu.make_async_remote_copy(
            src_ref=src.at[there, part], dst_ref=dst.at[slot, part],
            send_sem=send.at[chunk, there], recv_sem=recv.at[chunk, slot],
            device_id={"head": there}, device_id_type=MESH,
        )

    def kv_copy(there, slot):
        return pltpu.make_async_remote_copy(
            src_ref=kv_all.at[me_s], dst_ref=kv_all.at[slot],
            send_sem=kv_send.at[there], recv_sem=kv_recv.at[slot],
            device_id={"seq": there}, device_id_type=MESH,
        )

    partner = me_s + 1 - 2 * lax.rem(me_s, 2)

    def pass_copy(slot):
        return pltpu.make_async_remote_copy(
            src_ref=kv_all.at[slot], dst_ref=kv_all.at[slot],
            send_sem=pass_send.at[slot], recv_sem=kv_recv.at[slot],
            device_id={"seq": partner}, device_id_type=MESH,
        )

    def term_copy(group, kind, there, slot):
        send, recv = ((old_send, old_recv), (new_send, new_recv))[kind]
        return pltpu.make_async_remote_copy(
            src_ref=term_out.at[group, kind, there], dst_ref=term_in.at[group, kind, slot],
            send_sem=send.at[group, there], recv_sem=recv.at[group, slot],
            device_id={"seq": there}, device_id_type=MESH,
        )

    for kind, ref in enumerate((ko_ref, vo_ref, kn_ref, vn_ref)):
        kv_all[me_s, kind] = ref[...]

    barrier = pltpu.get_barrier_semaphore()
    for k in range(1, heads):
        pl.semaphore_signal(barrier, inc=1, device_id={"head": peer_h(k)}, device_id_type=MESH)
    for k in range(1, seqs):
        pl.semaphore_signal(barrier, inc=1, device_id={"seq": peer_s(k)}, device_id_type=MESH)
    pl.semaphore_wait(barrier, heads + seqs - 2)

    @pl.loop(1, seqs // 2)
    def _(k):
        kv_copy(peer_s(2 * k), me_s).start()

    kv_copy(partner, me_s).start()

    @pl.loop(0, chunks)
    def _(chunk):
        for k in range(1, heads):
            row_copy(q_ref, q_all, q_send, q_recv, chunk, peer_h(k), me_h).start()
            row_copy(do_ref, do_all, do_send, do_recv, chunk, peer_h(k), me_h).start()

    q_all[me_h] = q_ref[me_h]
    do_all[me_h] = do_ref[me_h]

    @pl.loop(1, seqs // 2)
    def _(k):
        slot = peer_s(2 * k)
        kv_copy(slot, slot).wait_recv()
        pass_copy(slot).start()

    @pl.loop(0, seqs // 2)
    def _(k):
        slot = lax.rem(partner + 2 * k, seqs)
        kv_copy(slot, slot).wait_recv()

    base = lax.rem(off_ref[0] + me_s * tokens, total)
    old_rows = total - me_s * tokens

    def slot_of(row):
        slot = row + base
        return jnp.where(slot >= total, slot - total, slot)

    @pl.loop(0, seqs - me_s)
    def _(block):
        row = block * tokens + lax.broadcasted_iota(jnp.int32, (tokens, total), 0)
        slot = lax.broadcasted_iota(jnp.int32, (tokens, total), 1)
        pick = jnp.where(slot_of(row) == slot, 1.0, 0.0).astype(jnp.bfloat16)
        for kind in range(2):
            stored = kv_all[:, kind].reshape(total, groups * width)
            line[kind, pl.ds(block * tokens, tokens)] = dot(pick, stored, NN).astype(jnp.bfloat16)

    @pl.loop(0, me_s + 1)
    def _(block):
        for kind in range(2):
            line[kind, pl.ds((seqs - me_s + block) * tokens, tokens)] = kv_all[block, 2 + kind]

    for group in range(groups):
        left = group * width
        window = win_ref[group]
        place = lax.broadcasted_iota(jnp.int32, (span, tokens), 0) - total
        token = lax.broadcasted_iota(jnp.int32, (span, tokens), 1)
        bias[...] = jnp.where((place <= token) & (place > token - window), 0.0, -jnp.inf)
        keys_t[...] = line[0, :, left : left + width].T
        sums[...] = jnp.zeros_like(sums)

        @pl.loop(0, steps)
        def _(step):
            chunk = group * steps + step
            first = chunk * hb
            for k in range(1, heads):
                row_copy(q_ref, q_all, q_send, q_recv, chunk, peer_h(k), peer_h(k)).wait_recv()
                row_copy(do_ref, do_all, do_send, do_recv, chunk, peer_h(k), peer_h(k)).wait_recv()
            q = jnp.concatenate([q_all[:, first + h].reshape(tokens, width) for h in range(hb)], 0)
            do = jnp.concatenate([do_all[:, first + h].reshape(tokens, width) for h in range(hb)], 0)
            keys = line[0, :, left : left + width]
            values = line[1, :, left : left + width]
            scores = dot(keys, q, NT) + jnp.concatenate([bias[...]] * hb, 1)
            top = jnp.max(scores, axis=0, keepdims=True)
            grown = jnp.exp2((scores - top) * (scale * math.log2(math.e)))
            inverse = 1.0 / jnp.sum(grown, axis=0, keepdims=True)
            weight_grad = dot(values, do, NT)
            delta = jnp.sum(grown * weight_grad, axis=0, keepdims=True) * inverse
            weights = grown * inverse
            dscore = (weights * (weight_grad - delta)).astype(jnp.bfloat16)
            dqt = dot(keys_t[...], dscore, NN) * scale
            for h in range(hb):
                piece = dqt[:, h * tokens : (h + 1) * tokens].T.astype(jnp.bfloat16)
                dq_out[:, first + h] = piece.reshape(heads, rows, width)
            for k in range(1, heads):
                row_copy(dq_out, dq_in, dq_send, dq_recv, chunk, peer_h(k), me_h).start()
            sums[:, :width] += dot(dscore, q, NN)
            sums[:, width:] += dot(weights.astype(jnp.bfloat16), do, NN)

        terms[:, :width] = (sums[:, :width] * scale).astype(jnp.bfloat16)
        terms[:, width:] = sums[:, width:].astype(jnp.bfloat16)

        @pl.loop(0, seqs)
        def _(k):
            there = peer_s(k)
            row = lax.broadcasted_iota(jnp.int32, (tokens, total), 1)
            slot = there * tokens + lax.broadcasted_iota(jnp.int32, (tokens, total), 0)
            chosen = (slot_of(row) == slot) & (row < old_rows)
            pick = jnp.where(chosen, 1.0, 0.0).astype(jnp.bfloat16)
            term_out[group, 0, there] = dot(pick, terms[:total], NN).astype(jnp.bfloat16)

            @pl.when(there <= me_s)
            def _():
                term_out[group, 1, there] = terms[pl.ds((seqs - me_s + there) * tokens, tokens)]

            @pl.when(k > 0)
            def _():
                term_copy(group, 0, there, me_s).start()

                @pl.when(there < me_s)
                def _():
                    term_copy(group, 1, there, me_s).start()

    for k in range(heads):
        there = peer_h(k)
        place = pl.ds(there * groups * per_group, groups * per_group)
        if k == 0:
            dq_ref[place] = dq_out[there]
            continue

        @pl.loop(0, chunks)
        def _(chunk):
            row_copy(dq_out, dq_in, dq_send, dq_recv, chunk, there, there).wait_recv()

        dq_ref[place] = dq_in[there]

    for group in range(groups):
        for kind in range(2):
            grad_ref[group, kind] = term_out[group, kind, me_s].astype(jnp.float32)

        @pl.loop(1, seqs)
        def _(k):
            there = peer_s(k)
            term_copy(group, 0, there, there).wait_recv()
            grad_ref[group, 0] += term_in[group, 0, there].astype(jnp.float32)

            @pl.when(there > me_s)
            def _():
                term_copy(group, 1, there, there).wait_recv()
                grad_ref[group, 1] += term_in[group, 1, there].astype(jnp.float32)

    kv_copy(partner, me_s).wait_send()

    @pl.loop(1, seqs // 2)
    def _(k):
        kv_copy(peer_s(2 * k), me_s).wait_send()
        pass_copy(peer_s(2 * k)).wait_send()

    @pl.loop(0, chunks)
    def _(chunk):
        for k in range(1, heads):
            row_copy(q_ref, q_all, q_send, q_recv, chunk, peer_h(k), me_h).wait_send()
            row_copy(do_ref, do_all, do_send, do_recv, chunk, peer_h(k), me_h).wait_send()
            row_copy(dq_out, dq_in, dq_send, dq_recv, chunk, peer_h(k), me_h).wait_send()

    @pl.loop(1, seqs)
    def _(k):
        there = peer_s(k)
        for group in range(groups):
            term_copy(group, 0, there, me_s).wait_send()

            @pl.when(there < me_s)
            def _():
                term_copy(group, 1, there, me_s).wait_send()


def kernel(
    heads, seqs, per_group, heads_at_once,
    win_ref, off_ref, q_ref, do_ref, kv_ref,
    dq_ref, grad_ref,
    wide, q_mine, do_mine, q_all, do_all, kv_all, line, keys_t, bias, sums, win_out, win_in,
    own_part, sib_out, sib_in, chip_sum, term_in, fold_in, fold_out, dq_out, dq_in,
    q_send, q_recv, do_send, do_recv, dq_send, dq_recv, win_sems,
    far_send, far_recv, plane_send, sib_send, kv_recv,
    part_send, part_recv, term_send, term_recv, fold_recv, back_send,
):
    hb = heads_at_once
    half = heads // 2
    chips = seqs // 2
    me_h, me_s = lax.axis_index("head"), lax.axis_index("seq")
    chip, side = me_s // 2, lax.rem(me_s, 2)
    sibling = chip * 2 + 1 - side
    pair, place = me_h // half, lax.rem(me_h, half)
    far_h = lax.rem(me_h + half, heads)
    rows, all_heads, width = q_ref.shape
    mine = all_heads // heads
    groups = mine // per_group
    tokens = rows * heads
    run = rows * half
    total = tokens * seqs
    span = total + run
    steps = per_group // hb
    scale = 1.0 / math.sqrt(width)
    first_token = me_s * tokens + pair * run
    narrow = jnp.bfloat16

    stages = [(0, 0)] + [(1, g) for g in range(groups)] + [(0, g) for g in range(1, groups)]
    stage_of = {key: at for at, key in enumerate(stages)}
    peers = []
    for dj in range(1, half):
        there = lax.rem(place + dj, half)
        peers.append((pair * half + there, there))

    def set_of(far, head):
        return lax.rem(head + half, heads) if far else head

    def chip_at(k):
        return lax.rem(chip + k, chips)

    def row_copy(src, dst, send, recv, stage, step, peer, from_slot, order):
        far, group = stages[stage]
        part = pl.ds(group * per_group + step * hb, hb)
        return pltpu.make_async_remote_copy(
            src_ref=src.at[from_slot, part], dst_ref=dst.at[far, place, part],
            send_sem=send.at[stage, step, peer[1]], recv_sem=recv.at[stage, step, order],
            device_id={"head": peer[0]}, device_id_type=MESH,
        )

    def q_copies(stage, step, peer, order):
        source = set_of(stages[stage][0], peer[0])
        return (
            row_copy(q_mine, q_all, q_send, q_recv, stage, step, peer, source, order),
            row_copy(do_mine, do_all, do_send, do_recv, stage, step, peer, source, order),
        )

    def dq_copy(stage, step, peer, order):
        far = stages[stage][0]
        return row_copy(dq_out.at[far], dq_in, dq_send, dq_recv, stage, step, peer, peer[1], order)

    def win_copy():
        return pltpu.make_async_remote_copy(
            src_ref=win_out, dst_ref=win_in, send_sem=win_sems.at[0], recv_sem=win_sems.at[1],
            device_id={"head": far_h}, device_id_type=MESH,
        )

    def far_copy(group):
        return pltpu.make_async_remote_copy(
            src_ref=kv_ref.at[group], dst_ref=kv_all.at[stage_of[1, group], me_s],
            send_sem=far_send.at[group], recv_sem=far_recv.at[group],
            device_id={"head": far_h}, device_id_type=MESH,
        )

    def plane_copy(stage, new, there):
        block = kv_all.at[stage, me_s, pl.ds(2 * new, 2)]
        return pltpu.make_async_remote_copy(
            src_ref=block, dst_ref=block,
            send_sem=plane_send.at[stage, new, there], recv_sem=kv_recv.at[stage, new, me_s],
            device_id={"seq": there * 2 + side}, device_id_type=MESH,
        )

    def sib_copy(stage, new, owner):
        block = kv_all.at[stage, owner, pl.ds(2 * new, 2)]
        return pltpu.make_async_remote_copy(
            src_ref=block, dst_ref=block,
            send_sem=sib_send.at[stage, new, owner // 2], recv_sem=kv_recv.at[stage, new, owner],
            device_id={"seq": sibling}, device_id_type=MESH,
        )

    def part_copy(stage, kind, there):
        return pltpu.make_async_remote_copy(
            src_ref=sib_out.at[stage, kind, there], dst_ref=sib_in.at[stage, kind, there],
            send_sem=part_send.at[stage, kind, there], recv_sem=part_recv.at[stage, kind, there],
            device_id={"seq": sibling}, device_id_type=MESH,
        )

    def term_copy(stage, kind, there, slot):
        far, group = stages[stage]
        dst, recv = (fold_in, fold_recv) if far else (term_in, term_recv)
        return pltpu.make_async_remote_copy(
            src_ref=chip_sum.at[stage, kind, there], dst_ref=dst.at[group, kind, slot],
            send_sem=term_send.at[stage, kind, there], recv_sem=recv.at[group, kind, slot],
            device_id={"seq": there * 2 + side}, device_id_type=MESH,
        )

    def back_copy(group, kind):
        return pltpu.make_async_remote_copy(
            src_ref=fold_out.at[group, kind], dst_ref=term_in.at[group, kind, chips],
            send_sem=back_send.at[group, kind], recv_sem=term_recv.at[group, kind, chips],
            device_id={"head": far_h}, device_id_type=MESH,
        )

    barrier = pltpu.get_barrier_semaphore()
    for k in range(1, heads):
        pl.semaphore_signal(barrier, inc=1, device_id={"head": lax.rem(me_h + k, heads)}, device_id_type=MESH)
    for k in range(1, chips):
        pl.semaphore_signal(barrier, inc=1, device_id={"seq": chip_at(k) * 2 + side}, device_id_type=MESH)
    pl.semaphore_signal(barrier, inc=1, device_id={"seq": sibling}, device_id_type=MESH)

    for ref, out in ((q_ref, q_mine), (do_ref, do_mine)):
        wide[...] = ref[...].astype(jnp.float32).reshape(rows * all_heads, width)
        for head in range(all_heads):
            out[head // mine, head % mine] = wide[pl.ds(head, rows, stride=all_heads)].astype(narrow)
    for group in range(groups):
        win_out[group] = jnp.full(win_out.shape[1:], win_ref[group], jnp.int32)
        kv_all[stage_of[0, group], me_s] = kv_ref[group]

    pl.semaphore_wait(barrier, heads - 1 + chips - 1 + 1)

    def share(stage):
        for new in range(2):
            @pl.loop(1, chips)
            def _(k):
                @pl.when((chip_at(k) >= chip) | (new == 0))
                def _():
                    plane_copy(stage, new, chip_at(k)).start()

            sib_copy(stage, new, me_s).start()

    def relay(stage):
        far_copy(stages[stage][1]).wait_recv()
        share(stage)

    def service(stage):
        @pl.loop(1, chips)
        def _(k):
            there = chip_at(k)
            owner = there * 2 + side
            for new in range(2):
                @pl.when((there <= chip) | (new == 0))
                def _():
                    sib_copy(stage, new, owner).wait_recv()
                    sib_copy(stage, new, owner).start()

    def settle(stage):
        @pl.loop(0, chips)
        def _(there):
            owner = there * 2 + 1 - side
            for new in range(2):
                @pl.when((there <= chip) | (new == 0))
                def _():
                    sib_copy(stage, new, owner).wait_recv()

    def send_rows(stage):
        @pl.loop(0, steps)
        def _(step):
            for peer in peers:
                for copy in q_copies(stage, step, peer, place):
                    copy.start()

    far_copy(0).start()
    win_copy().start()
    share(0)
    send_rows(0)
    for group in range(1, groups):
        far_copy(group).start()
    for stage in range(1, len(stages)):
        send_rows(stage)

    for far in range(2):
        q_all[far, place] = q_mine[set_of(far, me_h)]
        do_all[far, place] = do_mine[set_of(far, me_h)]

    old_rows = pl.multiple_of(total - first_token, run)
    base = lax.rem(off_ref[0] + first_token, total)

    def build(stage):
        for kind in range(2):
            @pl.loop(0, seqs)
            def _(owner):
                sums[kind, pl.ds(owner * tokens, tokens)] = kv_all[stage, owner, kind].astype(jnp.float32)

            sums[kind, total : total + tokens] = sums[kind, :tokens]

            @pl.loop(0, (old_rows + tokens - 1) // tokens)
            def _(block):
                start = lax.rem(base + block * tokens, total)
                line[kind, pl.ds(pl.multiple_of(block * tokens, tokens), tokens)] = sums[
                    kind, pl.ds(start, tokens)
                ].astype(narrow)

            @pl.loop(0, me_s + 1)
            def _(block):
                line[kind, pl.ds(pl.multiple_of(old_rows + block * tokens, run), tokens)] = kv_all[stage, block, 2 + kind]

        far, group = stages[stage]
        window = (win_in if far else win_out)[group, :1]
        position = lax.broadcasted_iota(jnp.int32, bias.shape, 0) - total
        token = lax.rem(lax.broadcasted_iota(jnp.int32, bias.shape, 1), run)
        bias[...] = jnp.where((position <= token) & (position > token - window), 0.0, -jnp.inf)
        keys_t[...] = line[0, :span].T
        sums[...] = jnp.zeros_like(sums)

    def attend(stage, step):
        far, group = stages[stage]
        first = group * per_group + step * hb
        for peer in peers:
            for copy in q_copies(stage, step, peer, peer[1]):
                copy.wait_recv()
        q = jnp.concatenate([q_all[far, :, first + h].reshape(run, width) for h in range(hb)], 0)
        do = jnp.concatenate([do_all[far, :, first + h].reshape(run, width) for h in range(hb)], 0)
        scores = dot(line[0, :span], q, NT) + jnp.concatenate([bias[...]] * (hb * run // bias.shape[1]), 1)
        top = jnp.max(scores, axis=0, keepdims=True)
        grown = jnp.exp2((scores - top) * (scale * math.log2(math.e)))
        inverse = 1.0 / jnp.sum(grown, axis=0, keepdims=True)
        weight_grad = dot(line[1, :span], do, NT)
        delta = jnp.sum(grown * weight_grad, axis=0, keepdims=True) * inverse
        weights = grown * inverse
        dscore = (weights * (weight_grad - delta)).astype(narrow)
        dqt = dot(keys_t[...], dscore, NN) * scale
        for h in range(0, hb, 2):
            piece = dqt[:, h * run : (h + 2) * run].T.astype(narrow).reshape(2, half, rows, width)
            for k in range(2):
                dq_out[far, :, first + h + k] = piece[k]
        for peer in peers:
            dq_copy(stage, step, peer, place).start()
        sums[0, :span] += dot(dscore, q, NN)
        sums[1, :span] += dot(weights.astype(narrow), do, NN)

    def put(stage, kind, there, seq_side, load):
        k_part = load(0) * scale
        v_part = load(1)

        @pl.when(seq_side == side)
        def _():
            own_part[kind, there, :, :width] = k_part
            own_part[kind, there, :, width:] = v_part

        @pl.when(seq_side != side)
        def _():
            sib_out[stage, kind, there, :, :width] = k_part.astype(narrow)
            sib_out[stage, kind, there, :, width:] = v_part.astype(narrow)
            part_copy(stage, kind, there).start()

    def split(stage):
        @pl.loop(0, 2 * chip + 2)
        def _(block):
            part = pl.ds(pl.multiple_of(old_rows + block * tokens, run), tokens)
            put(stage, 1, block // 2, lax.rem(block, 2), lambda i: sums[i, part])

        @pl.loop(old_rows // run, total // run)
        def _(block):
            for kind in range(2):
                sums[kind, pl.ds(pl.multiple_of(block * run, run), run)] = jnp.zeros((run, width), jnp.float32)

        for kind in range(2):
            sums[kind, total : total + tokens] = sums[kind, :tokens]

        @pl.loop(0, seqs)
        def _(block):
            start = lax.rem(block * tokens + total - base, total)
            put(stage, 0, block // 2, lax.rem(block, 2), lambda i: sums[i, pl.ds(start, tokens)])

    def finish(stage):
        for kind in range(2):
            @pl.loop(0, chips)
            def _(k):
                there = chip_at(k + 1)

                @pl.when((there <= chip) | (kind == 0))
                def _():
                    part_copy(stage, kind, there).wait_recv()
                    both = own_part[kind, there] + sib_in[stage, kind, there].astype(jnp.float32)
                    chip_sum[stage, kind, there] = both.astype(narrow)

                    @pl.when(there != chip)
                    def _():
                        term_copy(stage, kind, there, chip).start()

    def gather(stage, kind):
        far, group = stages[stage]
        source = fold_in if far else term_in
        own_part[kind, 0] = chip_sum[stage, kind, chip].astype(jnp.float32)

        @pl.loop(1, chips)
        def _(k):
            there = chip_at(k)

            @pl.when((there >= chip) | (kind == 0))
            def _():
                term_copy(stage, kind, there, there).wait_recv()
                own_part[kind, 0] += source[group, kind, there].astype(jnp.float32)

    def fold(stage):
        group = stages[stage][1]
        for kind in range(2):
            gather(stage, kind)
            fold_out[group, kind] = own_part[kind, 0].astype(narrow)
            back_copy(group, kind).start()

    last = len(stages) - 1
    relay(1)
    service(0)
    settle(0)
    win_copy().wait_recv()
    for stage in range(last + 1):
        build(stage)

        @pl.loop(0, steps)
        def _(step):
            @pl.when(step == steps - 1)
            def _():
                if stage == 0:
                    for later in range(2, groups + 1):
                        relay(later)
                    for later in range(groups + 1, last + 1):
                        share(later)
                if stage > 0:
                    finish(stage - 1)
                if stage < last:
                    service(stage + 1)

            attend(stage, step)

        split(stage)
        if stage < last:
            settle(stage + 1)

    finish(last)
    for group in range(groups):
        fold(stage_of[1, group])

    for far in range(2):
        dq_ref[pl.ds(set_of(far, me_h) * mine, mine)] = dq_out[far, place]
        for peer in peers:
            for group in range(groups):
                @pl.loop(0, steps)
                def _(step):
                    dq_copy(stage_of[far, group], step, peer, peer[1]).wait_recv()

            dq_ref[pl.ds(set_of(far, peer[0]) * mine, mine)] = dq_in[far, peer[1]]

    for group in range(groups):
        for kind in range(2):
            gather(stage_of[0, group], kind)
            back_copy(group, kind).wait_recv()
            own_part[kind, 0] += term_in[group, kind, chips].astype(jnp.float32)
            for part in range(2):
                grad_ref[kind * 2 + part, pl.ds(group, tokens, stride=groups)] = own_part[
                    kind, 0, :, part * width : (part + 1) * width
                ]

    win_copy().wait_send()
    for group in range(groups):
        far_copy(group).wait_send()
        for kind in range(2):
            back_copy(group, kind).wait_send()
    for stage in range(last + 1):
        @pl.loop(0, steps)
        def _(step):
            for peer in peers:
                for copy in q_copies(stage, step, peer, place):
                    copy.wait_send()
                dq_copy(stage, step, peer, place).wait_send()

        for kind in range(2):
            sib_copy(stage, kind, me_s).wait_send()

            @pl.loop(1, chips)
            def _(k):
                there = chip_at(k)

                @pl.when((there >= chip) | (kind == 0))
                def _():
                    plane_copy(stage, kind, there).wait_send()

                @pl.when((there <= chip) | (kind == 0))
                def _():
                    sib_copy(stage, kind, there * 2 + side).wait_send()
                    term_copy(stage, kind, there, chip).wait_send()

            @pl.loop(0, chips)
            def _(there):
                @pl.when((there <= chip) | (kind == 0))
                def _():
                    part_copy(stage, kind, there).wait_send()


def plain_shards(query, key_new, value_new, key_old, value_old, offset, windows, grad_out):
    heads, seqs = lax.axis_size("head"), lax.axis_size("seq")
    rows, all_heads, width = query.shape
    tokens = rows * heads
    total = tokens * seqs
    groups = key_new.shape[1]
    span = total + tokens
    mine = all_heads // heads
    per_group = mine // groups
    hb = max(h for h in (1, 2, 4) if per_group % h == 0 and (h <= 1 or h * tokens * span <= 700_000))
    chunks = mine // hb

    def by_head(x):
        return x.transpose(1, 0, 2).reshape(heads, mine, rows, width)

    kv = [x.reshape(tokens, groups * width) for x in (key_old, value_old, key_new, value_new)]
    vmem = pl.BlockSpec(memory_space=pltpu.VMEM)
    smem = pl.BlockSpec(memory_space=pltpu.SMEM)
    narrow, wide = jnp.bfloat16, jnp.float32
    row_shape = (heads, mine, rows, width)
    row_sems = pltpu.SemaphoreType.DMA((chunks, heads))
    seq_sems = pltpu.SemaphoreType.DMA((seqs,))
    term_sems = pltpu.SemaphoreType.DMA((groups, seqs))
    term_shape = (groups, 2, seqs, tokens, 2 * width)
    dq, grads = pl.pallas_call(
        functools.partial(plain_kernel, heads, seqs, per_group, hb),
        in_specs=[smem, smem] + [vmem] * 6,
        out_specs=[vmem, vmem],
        out_shape=[
            jax.ShapeDtypeStruct((all_heads, rows, width), narrow),
            jax.ShapeDtypeStruct((groups, 2, tokens, 2 * width), wide),
        ],
        scratch_shapes=[
            pltpu.VMEM(row_shape, narrow),
            pltpu.VMEM(row_shape, narrow),
            pltpu.VMEM((seqs, 4, tokens, groups * width), narrow),
            pltpu.VMEM((2, span, groups * width), narrow),
            pltpu.VMEM((width, span), narrow),
            pltpu.VMEM((span, tokens), wide),
            pltpu.VMEM((span, 2 * width), wide),
            pltpu.VMEM((span, 2 * width), narrow),
            pltpu.VMEM(term_shape, narrow),
            pltpu.VMEM(term_shape, narrow),
            pltpu.VMEM(row_shape, narrow),
            pltpu.VMEM(row_shape, narrow),
            row_sems, row_sems, row_sems, row_sems, seq_sems, seq_sems, seq_sems,
            row_sems, row_sems, term_sems, term_sems, term_sems, term_sems,
        ],
        compiler_params=pltpu.CompilerParams(
            collective_id=0, has_side_effects=True, vmem_limit_bytes=62 * 2**20
        ),
    )(windows, offset, by_head(query), by_head(grad_out), *kv)
    grad_query = lax.optimization_barrier(dq.transpose(1, 0, 2)).astype(wide)
    grads = grads.reshape(groups, 2, tokens, 2, width).transpose(1, 3, 2, 0, 4)
    return (grad_query, grads[1, 0], grads[1, 1], grads[0, 0], grads[0, 1])


def shards(query, key_new, value_new, key_old, value_old, offset, windows, grad_out):
    heads, seqs = lax.axis_size("head"), lax.axis_size("seq")
    rows, all_heads, width = query.shape
    tokens = rows * heads
    total = tokens * seqs
    groups = key_new.shape[1]
    chips = seqs // 2
    half = heads // 2
    run = tokens // 2
    span = total + run
    padded = total + 2 * tokens
    mine = all_heads // heads
    per_group = mine // groups
    stages = 2 * groups
    budget = 60 * 2**20
    kept = total * width * (20 * stages + 8 * groups + 8) + 16 * padded * width + 20 * all_heads * rows * width
    fits = [h for h in (2, 4, 6) if per_group % h == 0 and 14 * h * run * span + kept < budget]
    if not fits or heads % 2 or seqs % 2:
        return plain_shards(query, key_new, value_new, key_old, value_old, offset, windows, grad_out)
    hb = max(fits)
    steps = per_group // hb

    kv = jnp.stack([key_old, value_old, key_new, value_new]).transpose(2, 0, 1, 3)
    vmem = pl.BlockSpec(memory_space=pltpu.VMEM)
    smem = pl.BlockSpec(memory_space=pltpu.SMEM)
    narrow, wide = jnp.bfloat16, jnp.float32
    row_shape = (heads, mine, rows, width)
    set_shape = (2, half, mine, rows, width)
    block = (tokens, 2 * width)
    dma = pltpu.SemaphoreType.DMA
    row_sems = dma((stages, steps, half))
    dq, grads = pl.pallas_call(
        functools.partial(kernel, heads, seqs, per_group, hb),
        in_specs=[smem, smem] + [vmem] * 3,
        out_specs=[vmem, vmem],
        out_shape=[
            jax.ShapeDtypeStruct((all_heads, rows, width), narrow),
            jax.ShapeDtypeStruct((4, tokens * groups, width), wide),
        ],
        scratch_shapes=[
            pltpu.VMEM((rows * all_heads, width), wide),
            pltpu.VMEM(row_shape, narrow),
            pltpu.VMEM(row_shape, narrow),
            pltpu.VMEM(set_shape, narrow),
            pltpu.VMEM(set_shape, narrow),
            pltpu.VMEM((stages, seqs, 4, tokens, width), narrow),
            pltpu.VMEM((2, padded, width), narrow),
            pltpu.VMEM((width, span), narrow),
            pltpu.VMEM((span, 2 * run), wide),
            pltpu.VMEM((2, padded, width), wide),
            pltpu.VMEM((groups, 8, 2 * run), jnp.int32),
            pltpu.VMEM((groups, 8, 2 * run), jnp.int32),
            pltpu.VMEM((2, chips) + block, wide),
            pltpu.VMEM((stages, 2, chips) + block, narrow),
            pltpu.VMEM((stages, 2, chips) + block, narrow),
            pltpu.VMEM((stages, 2, chips) + block, narrow),
            pltpu.VMEM((groups, 2, chips + 1) + block, narrow),
            pltpu.VMEM((groups, 2, chips) + block, narrow),
            pltpu.VMEM((groups, 2) + block, narrow),
            pltpu.VMEM(set_shape, narrow),
            pltpu.VMEM(set_shape, narrow),
            row_sems, row_sems, row_sems, row_sems, row_sems, row_sems, dma((2,)),
            dma((groups,)), dma((groups,)), dma((stages, 2, chips)), dma((stages, 2, chips)), dma((stages, 2, seqs)),
            dma((stages, 2, chips)), dma((stages, 2, chips)), dma((stages, 2, chips)),
            dma((groups, 2, chips + 1)), dma((groups, 2, chips)), dma((groups, 2)),
        ],
        compiler_params=pltpu.CompilerParams(
            collective_id=0, has_side_effects=True, vmem_limit_bytes=62 * 2**20
        ),
    )(windows, offset, query, grad_out, kv)
    grad_query = lax.optimization_barrier(dq.transpose(1, 0, 2)).astype(wide)
    grads = grads.reshape(4, tokens, groups, width)
    return (grad_query, grads[2], grads[3], grads[0], grads[1])


def solution(mesh):
    tokens = P(("seq", "head"), None, None)
    slots = P("seq", "head", None)
    return jax.shard_map(
        shards,
        mesh=mesh,
        in_specs=(tokens, slots, slots, slots, slots, P(), P("head"), tokens),
        out_specs=(tokens, slots, slots, slots, slots),
        check_vma=False,
    )
```

```python
import functools
import math

import jax
import jax.numpy as jnp
from jax import lax
from jax.experimental import pallas as pl
from jax.experimental.pallas import tpu as pltpu
from jax.sharding import PartitionSpec as P

MESH = pl.DeviceIdType.MESH
NT = (((1,), (1,)), ((), ()))
NN = (((1,), (0,)), ((), ()))


def dot(a, b, dims):
    return lax.dot_general(a, b, dims, preferred_element_type=jnp.float32)


def plain_kernel(
    heads, seqs, per_group, heads_at_once,
    win_ref, off_ref, q_ref, do_ref, ko_ref, vo_ref, kn_ref, vn_ref,
    dq_ref, grad_ref,
    q_all, do_all, kv_all, line, keys_t, bias, sums, terms, term_out, term_in, dq_out, dq_in,
    q_send, q_recv, do_send, do_recv, kv_send, kv_recv, pass_send, dq_send, dq_recv, old_send, old_recv, new_send, new_recv,
):
    hb = heads_at_once
    me_h, me_s = lax.axis_index("head"), lax.axis_index("seq")
    rows, width = q_ref.shape[2:]
    tokens = rows * heads
    groups = q_ref.shape[1] // per_group
    total = tokens * seqs
    span = total + tokens
    steps = per_group // hb
    chunks = groups * steps
    scale = 1.0 / math.sqrt(width)

    def peer_h(k):
        return lax.rem(me_h + k, heads)

    def peer_s(k):
        return lax.rem(me_s + k, seqs)

    def row_copy(src, dst, send, recv, chunk, there, slot):
        part = pl.ds(chunk * hb, hb)
        return pltpu.make_async_remote_copy(
            src_ref=src.at[there, part], dst_ref=dst.at[slot, part],
            send_sem=send.at[chunk, there], recv_sem=recv.at[chunk, slot],
            device_id={"head": there}, device_id_type=MESH,
        )

    def kv_copy(there, slot):
        return pltpu.make_async_remote_copy(
            src_ref=kv_all.at[me_s], dst_ref=kv_all.at[slot],
            send_sem=kv_send.at[there], recv_sem=kv_recv.at[slot],
            device_id={"seq": there}, device_id_type=MESH,
        )

    partner = me_s + 1 - 2 * lax.rem(me_s, 2)

    def pass_copy(slot):
        return pltpu.make_async_remote_copy(
            src_ref=kv_all.at[slot], dst_ref=kv_all.at[slot],
            send_sem=pass_send.at[slot], recv_sem=kv_recv.at[slot],
            device_id={"seq": partner}, device_id_type=MESH,
        )

    def term_copy(group, kind, there, slot):
        send, recv = ((old_send, old_recv), (new_send, new_recv))[kind]
        return pltpu.make_async_remote_copy(
            src_ref=term_out.at[group, kind, there], dst_ref=term_in.at[group, kind, slot],
            send_sem=send.at[group, there], recv_sem=recv.at[group, slot],
            device_id={"seq": there}, device_id_type=MESH,
        )

    for kind, ref in enumerate((ko_ref, vo_ref, kn_ref, vn_ref)):
        kv_all[me_s, kind] = ref[...]

    barrier = pltpu.get_barrier_semaphore()
    for k in range(1, heads):
        pl.semaphore_signal(barrier, inc=1, device_id={"head": peer_h(k)}, device_id_type=MESH)
    for k in range(1, seqs):
        pl.semaphore_signal(barrier, inc=1, device_id={"seq": peer_s(k)}, device_id_type=MESH)
    pl.semaphore_wait(barrier, heads + seqs - 2)

    @pl.loop(1, seqs // 2)
    def _(k):
        kv_copy(peer_s(2 * k), me_s).start()

    kv_copy(partner, me_s).start()

    @pl.loop(0, chunks)
    def _(chunk):
        for k in range(1, heads):
            row_copy(q_ref, q_all, q_send, q_recv, chunk, peer_h(k), me_h).start()
            row_copy(do_ref, do_all, do_send, do_recv, chunk, peer_h(k), me_h).start()

    q_all[me_h] = q_ref[me_h]
    do_all[me_h] = do_ref[me_h]

    @pl.loop(1, seqs // 2)
    def _(k):
        slot = peer_s(2 * k)
        kv_copy(slot, slot).wait_recv()
        pass_copy(slot).start()

    @pl.loop(0, seqs // 2)
    def _(k):
        slot = lax.rem(partner + 2 * k, seqs)
        kv_copy(slot, slot).wait_recv()

    base = lax.rem(off_ref[0] + me_s * tokens, total)
    old_rows = total - me_s * tokens

    def slot_of(row):
        slot = row + base
        return jnp.where(slot >= total, slot - total, slot)

    @pl.loop(0, seqs - me_s)
    def _(block):
        row = block * tokens + lax.broadcasted_iota(jnp.int32, (tokens, total), 0)
        slot = lax.broadcasted_iota(jnp.int32, (tokens, total), 1)
        pick = jnp.where(slot_of(row) == slot, 1.0, 0.0).astype(jnp.bfloat16)
        for kind in range(2):
            stored = kv_all[:, kind].reshape(total, groups * width)
            line[kind, pl.ds(block * tokens, tokens)] = dot(pick, stored, NN).astype(jnp.bfloat16)

    @pl.loop(0, me_s + 1)
    def _(block):
        for kind in range(2):
            line[kind, pl.ds((seqs - me_s + block) * tokens, tokens)] = kv_all[block, 2 + kind]

    for group in range(groups):
        left = group * width
        window = win_ref[group]
        place = lax.broadcasted_iota(jnp.int32, (span, tokens), 0) - total
        token = lax.broadcasted_iota(jnp.int32, (span, tokens), 1)
        bias[...] = jnp.where((place <= token) & (place > token - window), 0.0, -jnp.inf)
        keys_t[...] = line[0, :, left : left + width].T
        sums[...] = jnp.zeros_like(sums)

        @pl.loop(0, steps)
        def _(step):
            chunk = group * steps + step
            first = chunk * hb
            for k in range(1, heads):
                row_copy(q_ref, q_all, q_send, q_recv, chunk, peer_h(k), peer_h(k)).wait_recv()
                row_copy(do_ref, do_all, do_send, do_recv, chunk, peer_h(k), peer_h(k)).wait_recv()
            q = jnp.concatenate([q_all[:, first + h].reshape(tokens, width) for h in range(hb)], 0)
            do = jnp.concatenate([do_all[:, first + h].reshape(tokens, width) for h in range(hb)], 0)
            keys = line[0, :, left : left + width]
            values = line[1, :, left : left + width]
            scores = dot(keys, q, NT) + jnp.concatenate([bias[...]] * hb, 1)
            top = jnp.max(scores, axis=0, keepdims=True)
            grown = jnp.exp2((scores - top) * (scale * math.log2(math.e)))
            inverse = 1.0 / jnp.sum(grown, axis=0, keepdims=True)
            weight_grad = dot(values, do, NT)
            delta = jnp.sum(grown * weight_grad, axis=0, keepdims=True) * inverse
            weights = grown * inverse
            dscore = (weights * (weight_grad - delta)).astype(jnp.bfloat16)
            dqt = dot(keys_t[...], dscore, NN) * scale
            for h in range(hb):
                piece = dqt[:, h * tokens : (h + 1) * tokens].T.astype(jnp.bfloat16)
                dq_out[:, first + h] = piece.reshape(heads, rows, width)
            for k in range(1, heads):
                row_copy(dq_out, dq_in, dq_send, dq_recv, chunk, peer_h(k), me_h).start()
            sums[:, :width] += dot(dscore, q, NN)
            sums[:, width:] += dot(weights.astype(jnp.bfloat16), do, NN)

        terms[:, :width] = (sums[:, :width] * scale).astype(jnp.bfloat16)
        terms[:, width:] = sums[:, width:].astype(jnp.bfloat16)

        @pl.loop(0, seqs)
        def _(k):
            there = peer_s(k)
            row = lax.broadcasted_iota(jnp.int32, (tokens, total), 1)
            slot = there * tokens + lax.broadcasted_iota(jnp.int32, (tokens, total), 0)
            chosen = (slot_of(row) == slot) & (row < old_rows)
            pick = jnp.where(chosen, 1.0, 0.0).astype(jnp.bfloat16)
            term_out[group, 0, there] = dot(pick, terms[:total], NN).astype(jnp.bfloat16)

            @pl.when(there <= me_s)
            def _():
                term_out[group, 1, there] = terms[pl.ds((seqs - me_s + there) * tokens, tokens)]

            @pl.when(k > 0)
            def _():
                term_copy(group, 0, there, me_s).start()

                @pl.when(there < me_s)
                def _():
                    term_copy(group, 1, there, me_s).start()

    for k in range(heads):
        there = peer_h(k)
        place = pl.ds(there * groups * per_group, groups * per_group)
        if k == 0:
            dq_ref[place] = dq_out[there]
            continue

        @pl.loop(0, chunks)
        def _(chunk):
            row_copy(dq_out, dq_in, dq_send, dq_recv, chunk, there, there).wait_recv()

        dq_ref[place] = dq_in[there]

    for group in range(groups):
        for kind in range(2):
            grad_ref[group, kind] = term_out[group, kind, me_s].astype(jnp.float32)

        @pl.loop(1, seqs)
        def _(k):
            there = peer_s(k)
            term_copy(group, 0, there, there).wait_recv()
            grad_ref[group, 0] += term_in[group, 0, there].astype(jnp.float32)

            @pl.when(there > me_s)
            def _():
                term_copy(group, 1, there, there).wait_recv()
                grad_ref[group, 1] += term_in[group, 1, there].astype(jnp.float32)

    kv_copy(partner, me_s).wait_send()

    @pl.loop(1, seqs // 2)
    def _(k):
        kv_copy(peer_s(2 * k), me_s).wait_send()
        pass_copy(peer_s(2 * k)).wait_send()

    @pl.loop(0, chunks)
    def _(chunk):
        for k in range(1, heads):
            row_copy(q_ref, q_all, q_send, q_recv, chunk, peer_h(k), me_h).wait_send()
            row_copy(do_ref, do_all, do_send, do_recv, chunk, peer_h(k), me_h).wait_send()
            row_copy(dq_out, dq_in, dq_send, dq_recv, chunk, peer_h(k), me_h).wait_send()

    @pl.loop(1, seqs)
    def _(k):
        there = peer_s(k)
        for group in range(groups):
            term_copy(group, 0, there, me_s).wait_send()

            @pl.when(there < me_s)
            def _():
                term_copy(group, 1, there, me_s).wait_send()


def kernel(
    heads, seqs, per_group, heads_at_once,
    win_ref, off_ref, q_ref, do_ref, ko_ref, vo_ref, kn_ref, vn_ref,
    dq_ref, grad_ref,
    wide, q_mine, do_mine, q_all, do_all, kv_all, line, keys_t, bias, sums, win_out, win_in, kv_ref,
    own_part, sib_out, sib_in, chip_sum, term_in, fold_in, fold_out, dq_out, dq_in,
    q_send, q_recv, do_send, do_recv, dq_send, dq_recv, win_sems,
    far_send, far_recv, plane_send, sib_send, kv_recv,
    part_send, part_recv, term_send, term_recv, fold_recv, back_send,
):
    hb = heads_at_once
    half = heads // 2
    chips = seqs // 2
    me_h, me_s = lax.axis_index("head"), lax.axis_index("seq")
    chip, side = me_s // 2, lax.rem(me_s, 2)
    sibling = chip * 2 + 1 - side
    pair, place = me_h // half, lax.rem(me_h, half)
    far_h = lax.rem(me_h + half, heads)
    rows, all_heads, width = q_ref.shape
    mine = all_heads // heads
    groups = mine // per_group
    tokens = rows * heads
    run = rows * half
    total = tokens * seqs
    span = total + run
    steps = per_group // hb
    scale = 1.0 / math.sqrt(width)
    first_token = me_s * tokens + pair * run
    narrow = jnp.bfloat16

    stages = [(0, 0)] + [(1, g) for g in range(groups)] + [(0, g) for g in range(1, groups)]
    stage_of = {key: at for at, key in enumerate(stages)}
    peers = []
    for dj in range(1, half):
        there = lax.rem(place + dj, half)
        peers.append((pair * half + there, there))

    def set_of(far, head):
        return lax.rem(head + half, heads) if far else head

    def chip_at(k):
        return lax.rem(chip + k, chips)

    def row_copy(src, dst, send, recv, stage, step, peer, from_slot, order):
        far, group = stages[stage]
        part = pl.ds(group * per_group + step * hb, hb)
        return pltpu.make_async_remote_copy(
            src_ref=src.at[from_slot, part], dst_ref=dst.at[far, place, part],
            send_sem=send.at[stage, step, peer[1]], recv_sem=recv.at[stage, step, order],
            device_id={"head": peer[0]}, device_id_type=MESH,
        )

    def q_copies(stage, step, peer, order):
        source = set_of(stages[stage][0], peer[0])
        return (
            row_copy(q_mine, q_all, q_send, q_recv, stage, step, peer, source, order),
            row_copy(do_mine, do_all, do_send, do_recv, stage, step, peer, source, order),
        )

    def dq_copy(stage, step, peer, order):
        far = stages[stage][0]
        return row_copy(dq_out.at[far], dq_in, dq_send, dq_recv, stage, step, peer, peer[1], order)

    def win_copy():
        return pltpu.make_async_remote_copy(
            src_ref=win_out, dst_ref=win_in, send_sem=win_sems.at[0], recv_sem=win_sems.at[1],
            device_id={"head": far_h}, device_id_type=MESH,
        )

    def far_copy(group):
        return pltpu.make_async_remote_copy(
            src_ref=kv_ref.at[group], dst_ref=kv_all.at[stage_of[1, group], me_s],
            send_sem=far_send.at[group], recv_sem=far_recv.at[group],
            device_id={"head": far_h}, device_id_type=MESH,
        )

    def plane_copy(stage, new, there):
        block = kv_all.at[stage, me_s, pl.ds(2 * new, 2)]
        return pltpu.make_async_remote_copy(
            src_ref=block, dst_ref=block,
            send_sem=plane_send.at[stage, new, there], recv_sem=kv_recv.at[stage, new, me_s],
            device_id={"seq": there * 2 + side}, device_id_type=MESH,
        )

    def sib_copy(stage, new, owner):
        block = kv_all.at[stage, owner, pl.ds(2 * new, 2)]
        return pltpu.make_async_remote_copy(
            src_ref=block, dst_ref=block,
            send_sem=sib_send.at[stage, new, owner // 2], recv_sem=kv_recv.at[stage, new, owner],
            device_id={"seq": sibling}, device_id_type=MESH,
        )

    def part_copy(stage, kind, there):
        return pltpu.make_async_remote_copy(
            src_ref=sib_out.at[stage, kind, there], dst_ref=sib_in.at[stage, kind, there],
            send_sem=part_send.at[stage, kind, there], recv_sem=part_recv.at[stage, kind, there],
            device_id={"seq": sibling}, device_id_type=MESH,
        )

    def term_copy(stage, kind, there, slot):
        far, group = stages[stage]
        dst, recv = (fold_in, fold_recv) if far else (term_in, term_recv)
        return pltpu.make_async_remote_copy(
            src_ref=chip_sum.at[stage, kind, there], dst_ref=dst.at[group, kind, slot],
            send_sem=term_send.at[stage, kind, there], recv_sem=recv.at[group, kind, slot],
            device_id={"seq": there * 2 + side}, device_id_type=MESH,
        )

    def back_copy(group, kind):
        return pltpu.make_async_remote_copy(
            src_ref=fold_out.at[group, kind], dst_ref=term_in.at[group, kind, chips],
            send_sem=back_send.at[group, kind], recv_sem=term_recv.at[group, kind, chips],
            device_id={"head": far_h}, device_id_type=MESH,
        )

    barrier = pltpu.get_barrier_semaphore()
    for k in range(1, heads):
        pl.semaphore_signal(barrier, inc=1, device_id={"head": lax.rem(me_h + k, heads)}, device_id_type=MESH)
    for k in range(1, chips):
        pl.semaphore_signal(barrier, inc=1, device_id={"seq": chip_at(k) * 2 + side}, device_id_type=MESH)
    pl.semaphore_signal(barrier, inc=1, device_id={"seq": sibling}, device_id_type=MESH)

    for ref, out in ((q_ref, q_mine), (do_ref, do_mine)):
        wide[...] = ref[...].astype(jnp.float32).reshape(rows * all_heads, width)
        for head in range(all_heads):
            out[head // mine, head % mine] = wide[pl.ds(head, rows, stride=all_heads)].astype(narrow)
    for group in range(groups):
        win_out[group] = jnp.full(win_out.shape[1:], win_ref[group], jnp.int32)
        for kind, ref in enumerate((ko_ref, vo_ref, kn_ref, vn_ref)):
            kv_ref[group, kind] = ref[:, group]
        kv_all[stage_of[0, group], me_s] = kv_ref[group]

    pl.semaphore_wait(barrier, heads - 1 + chips - 1 + 1)

    def share(stage):
        for new in range(2):
            @pl.loop(1, chips)
            def _(k):
                @pl.when((chip_at(k) >= chip) | (new == 0))
                def _():
                    plane_copy(stage, new, chip_at(k)).start()

            sib_copy(stage, new, me_s).start()

    def relay(stage):
        far_copy(stages[stage][1]).wait_recv()
        share(stage)

    def service(stage):
        @pl.loop(1, chips)
        def _(k):
            there = chip_at(k)
            owner = there * 2 + side
            for new in range(2):
                @pl.when((there <= chip) | (new == 0))
                def _():
                    sib_copy(stage, new, owner).wait_recv()
                    sib_copy(stage, new, owner).start()

    def settle(stage):
        @pl.loop(0, chips)
        def _(there):
            owner = there * 2 + 1 - side
            for new in range(2):
                @pl.when((there <= chip) | (new == 0))
                def _():
                    sib_copy(stage, new, owner).wait_recv()

    def send_rows(stage):
        @pl.loop(0, steps)
        def _(step):
            for peer in peers:
                for copy in q_copies(stage, step, peer, place):
                    copy.start()

    far_copy(0).start()
    win_copy().start()
    share(0)
    send_rows(0)
    for group in range(1, groups):
        far_copy(group).start()
    for stage in range(1, len(stages)):
        send_rows(stage)

    for far in range(2):
        q_all[far, place] = q_mine[set_of(far, me_h)]
        do_all[far, place] = do_mine[set_of(far, me_h)]

    old_rows = pl.multiple_of(total - first_token, run)
    base = lax.rem(off_ref[0] + first_token, total)

    def build(stage):
        for kind in range(2):
            @pl.loop(0, seqs)
            def _(owner):
                sums[kind, pl.ds(owner * tokens, tokens)] = kv_all[stage, owner, kind].astype(jnp.float32)

            sums[kind, total : total + tokens] = sums[kind, :tokens]

            @pl.loop(0, (old_rows + tokens - 1) // tokens)
            def _(block):
                start = lax.rem(base + block * tokens, total)
                line[kind, pl.ds(pl.multiple_of(block * tokens, tokens), tokens)] = sums[
                    kind, pl.ds(start, tokens)
                ].astype(narrow)

            @pl.loop(0, me_s + 1)
            def _(block):
                line[kind, pl.ds(pl.multiple_of(old_rows + block * tokens, run), tokens)] = kv_all[stage, block, 2 + kind]

        far, group = stages[stage]
        window = (win_in if far else win_out)[group, :1]
        position = lax.broadcasted_iota(jnp.int32, bias.shape, 0) - total
        token = lax.rem(lax.broadcasted_iota(jnp.int32, bias.shape, 1), run)
        bias[...] = jnp.where((position <= token) & (position > token - window), 0.0, -jnp.inf)
        keys_t[...] = line[0, :span].T
        sums[...] = jnp.zeros_like(sums)

    def attend(stage, step):
        far, group = stages[stage]
        first = group * per_group + step * hb
        for peer in peers:
            for copy in q_copies(stage, step, peer, peer[1]):
                copy.wait_recv()
        q = jnp.concatenate([q_all[far, :, first + h].reshape(run, width) for h in range(hb)], 0)
        do = jnp.concatenate([do_all[far, :, first + h].reshape(run, width) for h in range(hb)], 0)
        scores = dot(line[0, :span], q, NT) + jnp.concatenate([bias[...]] * (hb * run // bias.shape[1]), 1)
        top = jnp.max(scores, axis=0, keepdims=True)
        grown = jnp.exp2((scores - top) * (scale * math.log2(math.e)))
        inverse = 1.0 / jnp.sum(grown, axis=0, keepdims=True)
        weight_grad = dot(line[1, :span], do, NT)
        delta = jnp.sum(grown * weight_grad, axis=0, keepdims=True) * inverse
        weights = grown * inverse
        dscore = (weights * (weight_grad - delta)).astype(narrow)
        dqt = dot(keys_t[...], dscore, NN) * scale
        for h in range(0, hb, 2):
            piece = dqt[:, h * run : (h + 2) * run].T.astype(narrow).reshape(2, half, rows, width)
            for k in range(2):
                dq_out[far, :, first + h + k] = piece[k]
        for peer in peers:
            dq_copy(stage, step, peer, place).start()
        sums[0, :span] += dot(dscore, q, NN)
        sums[1, :span] += dot(weights.astype(narrow), do, NN)

    def put(stage, kind, there, seq_side, load):
        k_part = load(0) * scale
        v_part = load(1)

        @pl.when(seq_side == side)
        def _():
            own_part[kind, there, :, :width] = k_part
            own_part[kind, there, :, width:] = v_part

        @pl.when(seq_side != side)
        def _():
            sib_out[stage, kind, there, :, :width] = k_part.astype(narrow)
            sib_out[stage, kind, there, :, width:] = v_part.astype(narrow)
            part_copy(stage, kind, there).start()

    def split(stage):
        @pl.loop(0, 2 * chip + 2)
        def _(block):
            part = pl.ds(pl.multiple_of(old_rows + block * tokens, run), tokens)
            put(stage, 1, block // 2, lax.rem(block, 2), lambda i: sums[i, part])

        @pl.loop(old_rows // run, total // run)
        def _(block):
            for kind in range(2):
                sums[kind, pl.ds(pl.multiple_of(block * run, run), run)] = jnp.zeros((run, width), jnp.float32)

        for kind in range(2):
            sums[kind, total : total + tokens] = sums[kind, :tokens]

        @pl.loop(0, seqs)
        def _(block):
            start = lax.rem(block * tokens + total - base, total)
            put(stage, 0, block // 2, lax.rem(block, 2), lambda i: sums[i, pl.ds(start, tokens)])

    def finish(stage):
        for kind in range(2):
            @pl.loop(0, chips)
            def _(k):
                there = chip_at(k + 1)

                @pl.when((there <= chip) | (kind == 0))
                def _():
                    part_copy(stage, kind, there).wait_recv()
                    both = own_part[kind, there] + sib_in[stage, kind, there].astype(jnp.float32)
                    chip_sum[stage, kind, there] = both.astype(narrow)

                    @pl.when(there != chip)
                    def _():
                        term_copy(stage, kind, there, chip).start()

    def gather(stage, kind):
        far, group = stages[stage]
        source = fold_in if far else term_in
        own_part[kind, 0] = chip_sum[stage, kind, chip].astype(jnp.float32)

        @pl.loop(1, chips)
        def _(k):
            there = chip_at(k)

            @pl.when((there >= chip) | (kind == 0))
            def _():
                term_copy(stage, kind, there, there).wait_recv()
                own_part[kind, 0] += source[group, kind, there].astype(jnp.float32)

    def fold(stage):
        group = stages[stage][1]
        for kind in range(2):
            gather(stage, kind)
            fold_out[group, kind] = own_part[kind, 0].astype(narrow)
            back_copy(group, kind).start()

    last = len(stages) - 1
    relay(1)
    service(0)
    settle(0)
    win_copy().wait_recv()
    for stage in range(last + 1):
        build(stage)

        @pl.loop(0, steps)
        def _(step):
            @pl.when(step == steps - 1)
            def _():
                if stage == 0:
                    for later in range(2, groups + 1):
                        relay(later)
                    for later in range(groups + 1, last + 1):
                        share(later)
                if stage > 0:
                    finish(stage - 1)
                if stage == last:
                    for group in range(groups - 1):
                        fold(stage_of[1, group])
                if stage < last:
                    service(stage + 1)

            attend(stage, step)

        split(stage)
        if stage < last:
            settle(stage + 1)

    finish(last)
    fold(stage_of[1, groups - 1])

    for far in range(2):
        dq_ref[pl.ds(set_of(far, me_h) * mine, mine)] = dq_out[far, place]
        for peer in peers:
            for group in range(groups):
                @pl.loop(0, steps)
                def _(step):
                    dq_copy(stage_of[far, group], step, peer, peer[1]).wait_recv()

            dq_ref[pl.ds(set_of(far, peer[0]) * mine, mine)] = dq_in[far, peer[1]]

    for group in range(groups):
        for kind in range(2):
            gather(stage_of[0, group], kind)
            back_copy(group, kind).wait_recv()
            own_part[kind, 0] += term_in[group, kind, chips].astype(jnp.float32)
            for part in range(2):
                grad_ref[kind * 2 + part, pl.ds(group, tokens, stride=groups)] = own_part[
                    kind, 0, :, part * width : (part + 1) * width
                ]

    win_copy().wait_send()
    for group in range(groups):
        far_copy(group).wait_send()
        for kind in range(2):
            back_copy(group, kind).wait_send()
    for stage in range(last + 1):
        @pl.loop(0, steps)
        def _(step):
            for peer in peers:
                for copy in q_copies(stage, step, peer, place):
                    copy.wait_send()
                dq_copy(stage, step, peer, place).wait_send()

        for kind in range(2):
            sib_copy(stage, kind, me_s).wait_send()

            @pl.loop(1, chips)
            def _(k):
                there = chip_at(k)

                @pl.when((there >= chip) | (kind == 0))
                def _():
                    plane_copy(stage, kind, there).wait_send()

                @pl.when((there <= chip) | (kind == 0))
                def _():
                    sib_copy(stage, kind, there * 2 + side).wait_send()
                    term_copy(stage, kind, there, chip).wait_send()

            @pl.loop(0, chips)
            def _(there):
                @pl.when((there <= chip) | (kind == 0))
                def _():
                    part_copy(stage, kind, there).wait_send()


def plain_shards(query, key_new, value_new, key_old, value_old, offset, windows, grad_out):
    heads, seqs = lax.axis_size("head"), lax.axis_size("seq")
    rows, all_heads, width = query.shape
    tokens = rows * heads
    total = tokens * seqs
    groups = key_new.shape[1]
    span = total + tokens
    mine = all_heads // heads
    per_group = mine // groups
    hb = max(h for h in (1, 2, 4) if per_group % h == 0 and (h <= 1 or h * tokens * span <= 700_000))
    chunks = mine // hb

    def by_head(x):
        return x.transpose(1, 0, 2).reshape(heads, mine, rows, width)

    kv = [x.reshape(tokens, groups * width) for x in (key_old, value_old, key_new, value_new)]
    vmem = pl.BlockSpec(memory_space=pltpu.VMEM)
    smem = pl.BlockSpec(memory_space=pltpu.SMEM)
    narrow, wide = jnp.bfloat16, jnp.float32
    row_shape = (heads, mine, rows, width)
    row_sems = pltpu.SemaphoreType.DMA((chunks, heads))
    seq_sems = pltpu.SemaphoreType.DMA((seqs,))
    term_sems = pltpu.SemaphoreType.DMA((groups, seqs))
    term_shape = (groups, 2, seqs, tokens, 2 * width)
    dq, grads = pl.pallas_call(
        functools.partial(plain_kernel, heads, seqs, per_group, hb),
        in_specs=[smem, smem] + [vmem] * 6,
        out_specs=[vmem, vmem],
        out_shape=[
            jax.ShapeDtypeStruct((all_heads, rows, width), narrow),
            jax.ShapeDtypeStruct((groups, 2, tokens, 2 * width), wide),
        ],
        scratch_shapes=[
            pltpu.VMEM(row_shape, narrow),
            pltpu.VMEM(row_shape, narrow),
            pltpu.VMEM((seqs, 4, tokens, groups * width), narrow),
            pltpu.VMEM((2, span, groups * width), narrow),
            pltpu.VMEM((width, span), narrow),
            pltpu.VMEM((span, tokens), wide),
            pltpu.VMEM((span, 2 * width), wide),
            pltpu.VMEM((span, 2 * width), narrow),
            pltpu.VMEM(term_shape, narrow),
            pltpu.VMEM(term_shape, narrow),
            pltpu.VMEM(row_shape, narrow),
            pltpu.VMEM(row_shape, narrow),
            row_sems, row_sems, row_sems, row_sems, seq_sems, seq_sems, seq_sems,
            row_sems, row_sems, term_sems, term_sems, term_sems, term_sems,
        ],
        compiler_params=pltpu.CompilerParams(
            collective_id=0, has_side_effects=True, vmem_limit_bytes=62 * 2**20
        ),
    )(windows, offset, by_head(query), by_head(grad_out), *kv)
    grad_query = lax.optimization_barrier(dq.transpose(1, 0, 2)).astype(wide)
    grads = grads.reshape(groups, 2, tokens, 2, width).transpose(1, 3, 2, 0, 4)
    return (grad_query, grads[1, 0], grads[1, 1], grads[0, 0], grads[0, 1])


def shards(query, key_new, value_new, key_old, value_old, offset, windows, grad_out):
    heads, seqs = lax.axis_size("head"), lax.axis_size("seq")
    rows, all_heads, width = query.shape
    tokens = rows * heads
    total = tokens * seqs
    groups = key_new.shape[1]
    chips = seqs // 2
    half = heads // 2
    run = tokens // 2
    span = total + run
    padded = total + 2 * tokens
    mine = all_heads // heads
    per_group = mine // groups
    stages = 2 * groups
    budget = 60 * 2**20
    kept = total * width * (20 * stages + 8 * groups + 8) + 16 * padded * width + 20 * all_heads * rows * width
    fits = [h for h in (2, 4, 6) if per_group % h == 0 and 14 * h * run * span + kept < budget]
    if not fits or heads % 2 or seqs % 2:
        return plain_shards(query, key_new, value_new, key_old, value_old, offset, windows, grad_out)
    hb = max(fits)
    steps = per_group // hb

    vmem = pl.BlockSpec(memory_space=pltpu.VMEM)
    smem = pl.BlockSpec(memory_space=pltpu.SMEM)
    narrow, wide = jnp.bfloat16, jnp.float32
    row_shape = (heads, mine, rows, width)
    set_shape = (2, half, mine, rows, width)
    block = (tokens, 2 * width)
    dma = pltpu.SemaphoreType.DMA
    row_sems = dma((stages, steps, half))
    dq, grads = pl.pallas_call(
        functools.partial(kernel, heads, seqs, per_group, hb),
        in_specs=[smem, smem] + [vmem] * 6,
        out_specs=[vmem, vmem],
        out_shape=[
            jax.ShapeDtypeStruct((all_heads, rows, width), narrow),
            jax.ShapeDtypeStruct((4, tokens * groups, width), wide),
        ],
        scratch_shapes=[
            pltpu.VMEM((rows * all_heads, width), wide),
            pltpu.VMEM(row_shape, narrow),
            pltpu.VMEM(row_shape, narrow),
            pltpu.VMEM(set_shape, narrow),
            pltpu.VMEM(set_shape, narrow),
            pltpu.VMEM((stages, seqs, 4, tokens, width), narrow),
            pltpu.VMEM((2, padded, width), narrow),
            pltpu.VMEM((width, span), narrow),
            pltpu.VMEM((span, 2 * run), wide),
            pltpu.VMEM((2, padded, width), wide),
            pltpu.VMEM((groups, 8, 2 * run), jnp.int32),
            pltpu.VMEM((groups, 8, 2 * run), jnp.int32),
            pltpu.VMEM((groups, 4, tokens, width), narrow),
            pltpu.VMEM((2, chips) + block, wide),
            pltpu.VMEM((stages, 2, chips) + block, narrow),
            pltpu.VMEM((stages, 2, chips) + block, narrow),
            pltpu.VMEM((stages, 2, chips) + block, narrow),
            pltpu.VMEM((groups, 2, chips + 1) + block, narrow),
            pltpu.VMEM((groups, 2, chips) + block, narrow),
            pltpu.VMEM((groups, 2) + block, narrow),
            pltpu.VMEM(set_shape, narrow),
            pltpu.VMEM(set_shape, narrow),
            row_sems, row_sems, row_sems, row_sems, row_sems, row_sems, dma((2,)),
            dma((groups,)), dma((groups,)), dma((stages, 2, chips)), dma((stages, 2, chips)), dma((stages, 2, seqs)),
            dma((stages, 2, chips)), dma((stages, 2, chips)), dma((stages, 2, chips)),
            dma((groups, 2, chips + 1)), dma((groups, 2, chips)), dma((groups, 2)),
        ],
        compiler_params=pltpu.CompilerParams(
            collective_id=0, has_side_effects=True, vmem_limit_bytes=62 * 2**20
        ),
    )(windows, offset, query, grad_out, key_old, value_old, key_new, value_new)
    grad_query = lax.optimization_barrier(dq.transpose(1, 0, 2)).astype(wide)
    grads = grads.reshape(4, tokens, groups, width)
    return (grad_query, grads[2], grads[3], grads[0], grads[1])


def solution(mesh):
    tokens = P(("seq", "head"), None, None)
    slots = P("seq", "head", None)
    return jax.shard_map(
        shards,
        mesh=mesh,
        in_specs=(tokens, slots, slots, slots, slots, P(), P("head"), tokens),
        out_specs=(tokens, slots, slots, slots, slots),
        check_vma=False,
    )
```

```python
import functools
import math

import jax
import jax.numpy as jnp
from jax import lax
from jax.experimental import pallas as pl
from jax.experimental.pallas import tpu as pltpu
from jax.sharding import PartitionSpec as P

MESH = pl.DeviceIdType.MESH
NT = (((1,), (1,)), ((), ()))
NN = (((1,), (0,)), ((), ()))


def dot(a, b, dims):
    return lax.dot_general(a, b, dims, preferred_element_type=jnp.float32)


def plain_kernel(
    heads, seqs, per_group, heads_at_once,
    win_ref, off_ref, q_ref, do_ref, ko_ref, vo_ref, kn_ref, vn_ref,
    dq_ref, grad_ref,
    q_all, do_all, kv_all, line, keys_t, bias, sums, terms, term_out, term_in, dq_out, dq_in,
    q_send, q_recv, do_send, do_recv, kv_send, kv_recv, pass_send, dq_send, dq_recv, old_send, old_recv, new_send, new_recv,
):
    hb = heads_at_once
    me_h, me_s = lax.axis_index("head"), lax.axis_index("seq")
    rows, width = q_ref.shape[2:]
    tokens = rows * heads
    groups = q_ref.shape[1] // per_group
    total = tokens * seqs
    span = total + tokens
    steps = per_group // hb
    chunks = groups * steps
    scale = 1.0 / math.sqrt(width)

    def peer_h(k):
        return lax.rem(me_h + k, heads)

    def peer_s(k):
        return lax.rem(me_s + k, seqs)

    def row_copy(src, dst, send, recv, chunk, there, slot):
        part = pl.ds(chunk * hb, hb)
        return pltpu.make_async_remote_copy(
            src_ref=src.at[there, part], dst_ref=dst.at[slot, part],
            send_sem=send.at[chunk, there], recv_sem=recv.at[chunk, slot],
            device_id={"head": there}, device_id_type=MESH,
        )

    def kv_copy(there, slot):
        return pltpu.make_async_remote_copy(
            src_ref=kv_all.at[me_s], dst_ref=kv_all.at[slot],
            send_sem=kv_send.at[there], recv_sem=kv_recv.at[slot],
            device_id={"seq": there}, device_id_type=MESH,
        )

    partner = me_s + 1 - 2 * lax.rem(me_s, 2)

    def pass_copy(slot):
        return pltpu.make_async_remote_copy(
            src_ref=kv_all.at[slot], dst_ref=kv_all.at[slot],
            send_sem=pass_send.at[slot], recv_sem=kv_recv.at[slot],
            device_id={"seq": partner}, device_id_type=MESH,
        )

    def term_copy(group, kind, there, slot):
        send, recv = ((old_send, old_recv), (new_send, new_recv))[kind]
        return pltpu.make_async_remote_copy(
            src_ref=term_out.at[group, kind, there], dst_ref=term_in.at[group, kind, slot],
            send_sem=send.at[group, there], recv_sem=recv.at[group, slot],
            device_id={"seq": there}, device_id_type=MESH,
        )

    for kind, ref in enumerate((ko_ref, vo_ref, kn_ref, vn_ref)):
        kv_all[me_s, kind] = ref[...]

    barrier = pltpu.get_barrier_semaphore()
    for k in range(1, heads):
        pl.semaphore_signal(barrier, inc=1, device_id={"head": peer_h(k)}, device_id_type=MESH)
    for k in range(1, seqs):
        pl.semaphore_signal(barrier, inc=1, device_id={"seq": peer_s(k)}, device_id_type=MESH)
    pl.semaphore_wait(barrier, heads + seqs - 2)

    @pl.loop(1, seqs // 2)
    def _(k):
        kv_copy(peer_s(2 * k), me_s).start()

    kv_copy(partner, me_s).start()

    @pl.loop(0, chunks)
    def _(chunk):
        for k in range(1, heads):
            row_copy(q_ref, q_all, q_send, q_recv, chunk, peer_h(k), me_h).start()
            row_copy(do_ref, do_all, do_send, do_recv, chunk, peer_h(k), me_h).start()

    q_all[me_h] = q_ref[me_h]
    do_all[me_h] = do_ref[me_h]

    @pl.loop(1, seqs // 2)
    def _(k):
        slot = peer_s(2 * k)
        kv_copy(slot, slot).wait_recv()
        pass_copy(slot).start()

    @pl.loop(0, seqs // 2)
    def _(k):
        slot = lax.rem(partner + 2 * k, seqs)
        kv_copy(slot, slot).wait_recv()

    base = lax.rem(off_ref[0] + me_s * tokens, total)
    old_rows = total - me_s * tokens

    def slot_of(row):
        slot = row + base
        return jnp.where(slot >= total, slot - total, slot)

    @pl.loop(0, seqs - me_s)
    def _(block):
        row = block * tokens + lax.broadcasted_iota(jnp.int32, (tokens, total), 0)
        slot = lax.broadcasted_iota(jnp.int32, (tokens, total), 1)
        pick = jnp.where(slot_of(row) == slot, 1.0, 0.0).astype(jnp.bfloat16)
        for kind in range(2):
            stored = kv_all[:, kind].reshape(total, groups * width)
            line[kind, pl.ds(block * tokens, tokens)] = dot(pick, stored, NN).astype(jnp.bfloat16)

    @pl.loop(0, me_s + 1)
    def _(block):
        for kind in range(2):
            line[kind, pl.ds((seqs - me_s + block) * tokens, tokens)] = kv_all[block, 2 + kind]

    for group in range(groups):
        left = group * width
        window = win_ref[group]
        place = lax.broadcasted_iota(jnp.int32, (span, tokens), 0) - total
        token = lax.broadcasted_iota(jnp.int32, (span, tokens), 1)
        bias[...] = jnp.where((place <= token) & (place > token - window), 0.0, -jnp.inf)
        keys_t[...] = line[0, :, left : left + width].T
        sums[...] = jnp.zeros_like(sums)

        @pl.loop(0, steps)
        def _(step):
            chunk = group * steps + step
            first = chunk * hb
            for k in range(1, heads):
                row_copy(q_ref, q_all, q_send, q_recv, chunk, peer_h(k), peer_h(k)).wait_recv()
                row_copy(do_ref, do_all, do_send, do_recv, chunk, peer_h(k), peer_h(k)).wait_recv()
            q = jnp.concatenate([q_all[:, first + h].reshape(tokens, width) for h in range(hb)], 0)
            do = jnp.concatenate([do_all[:, first + h].reshape(tokens, width) for h in range(hb)], 0)
            keys = line[0, :, left : left + width]
            values = line[1, :, left : left + width]
            scores = dot(keys, q, NT) + jnp.concatenate([bias[...]] * hb, 1)
            top = jnp.max(scores, axis=0, keepdims=True)
            grown = jnp.exp2((scores - top) * (scale * math.log2(math.e)))
            inverse = 1.0 / jnp.sum(grown, axis=0, keepdims=True)
            weight_grad = dot(values, do, NT)
            delta = jnp.sum(grown * weight_grad, axis=0, keepdims=True) * inverse
            weights = grown * inverse
            dscore = (weights * (weight_grad - delta)).astype(jnp.bfloat16)
            dqt = dot(keys_t[...], dscore, NN) * scale
            for h in range(hb):
                piece = dqt[:, h * tokens : (h + 1) * tokens].T.astype(jnp.bfloat16)
                dq_out[:, first + h] = piece.reshape(heads, rows, width)
            for k in range(1, heads):
                row_copy(dq_out, dq_in, dq_send, dq_recv, chunk, peer_h(k), me_h).start()
            sums[:, :width] += dot(dscore, q, NN)
            sums[:, width:] += dot(weights.astype(jnp.bfloat16), do, NN)

        terms[:, :width] = (sums[:, :width] * scale).astype(jnp.bfloat16)
        terms[:, width:] = sums[:, width:].astype(jnp.bfloat16)

        @pl.loop(0, seqs)
        def _(k):
            there = peer_s(k)
            row = lax.broadcasted_iota(jnp.int32, (tokens, total), 1)
            slot = there * tokens + lax.broadcasted_iota(jnp.int32, (tokens, total), 0)
            chosen = (slot_of(row) == slot) & (row < old_rows)
            pick = jnp.where(chosen, 1.0, 0.0).astype(jnp.bfloat16)
            term_out[group, 0, there] = dot(pick, terms[:total], NN).astype(jnp.bfloat16)

            @pl.when(there <= me_s)
            def _():
                term_out[group, 1, there] = terms[pl.ds((seqs - me_s + there) * tokens, tokens)]

            @pl.when(k > 0)
            def _():
                term_copy(group, 0, there, me_s).start()

                @pl.when(there < me_s)
                def _():
                    term_copy(group, 1, there, me_s).start()

    for k in range(heads):
        there = peer_h(k)
        place = pl.ds(there * groups * per_group, groups * per_group)
        if k == 0:
            dq_ref[place] = dq_out[there]
            continue

        @pl.loop(0, chunks)
        def _(chunk):
            row_copy(dq_out, dq_in, dq_send, dq_recv, chunk, there, there).wait_recv()

        dq_ref[place] = dq_in[there]

    for group in range(groups):
        for kind in range(2):
            grad_ref[group, kind] = term_out[group, kind, me_s].astype(jnp.float32)

        @pl.loop(1, seqs)
        def _(k):
            there = peer_s(k)
            term_copy(group, 0, there, there).wait_recv()
            grad_ref[group, 0] += term_in[group, 0, there].astype(jnp.float32)

            @pl.when(there > me_s)
            def _():
                term_copy(group, 1, there, there).wait_recv()
                grad_ref[group, 1] += term_in[group, 1, there].astype(jnp.float32)

    kv_copy(partner, me_s).wait_send()

    @pl.loop(1, seqs // 2)
    def _(k):
        kv_copy(peer_s(2 * k), me_s).wait_send()
        pass_copy(peer_s(2 * k)).wait_send()

    @pl.loop(0, chunks)
    def _(chunk):
        for k in range(1, heads):
            row_copy(q_ref, q_all, q_send, q_recv, chunk, peer_h(k), me_h).wait_send()
            row_copy(do_ref, do_all, do_send, do_recv, chunk, peer_h(k), me_h).wait_send()
            row_copy(dq_out, dq_in, dq_send, dq_recv, chunk, peer_h(k), me_h).wait_send()

    @pl.loop(1, seqs)
    def _(k):
        there = peer_s(k)
        for group in range(groups):
            term_copy(group, 0, there, me_s).wait_send()

            @pl.when(there < me_s)
            def _():
                term_copy(group, 1, there, me_s).wait_send()


def kernel(
    heads, seqs, per_group, heads_at_once,
    win_ref, off_ref, q_ref, do_ref, ko_ref, vo_ref, kn_ref, vn_ref,
    dq_ref, grad_ref,
    wide, q_mine, do_mine, q_all, do_all, kv_all, line, keys_t, bias, sums, win_out, win_in, kv_ref,
    own_part, sib_out, sib_in, chip_sum, term_in, fold_in, fold_out, dq_out, dq_in,
    q_send, q_recv, do_send, do_recv, dq_send, dq_recv, win_sems,
    far_send, far_recv, plane_send, sib_send, kv_recv,
    part_send, part_recv, term_send, term_recv, fold_recv, back_send,
):
    hb = heads_at_once
    half = heads // 2
    chips = seqs // 2
    me_h, me_s = lax.axis_index("head"), lax.axis_index("seq")
    chip, side = me_s // 2, lax.rem(me_s, 2)
    sibling = chip * 2 + 1 - side
    pair, place = me_h // half, lax.rem(me_h, half)
    far_h = lax.rem(me_h + half, heads)
    rows, all_heads, width = q_ref.shape
    mine = all_heads // heads
    groups = mine // per_group
    tokens = rows * heads
    run = rows * half
    total = tokens * seqs
    span = total + run
    steps = per_group // hb
    scale = 1.0 / math.sqrt(width)
    first_token = me_s * tokens + pair * run
    narrow = jnp.bfloat16

    stages = [(0, 0)] + [(1, g) for g in range(groups)] + [(0, g) for g in range(1, groups)]
    stage_of = {key: at for at, key in enumerate(stages)}
    peers = []
    for dj in range(1, half):
        there = lax.rem(place + dj, half)
        peers.append((pair * half + there, there))

    def set_of(far, head):
        return lax.rem(head + half, heads) if far else head

    def chip_at(k):
        return lax.rem(chip + k, chips)

    def row_copy(src, dst, send, recv, stage, step, peer, from_slot, order):
        far, group = stages[stage]
        part = pl.ds(group * per_group + step * hb, hb)
        return pltpu.make_async_remote_copy(
            src_ref=src.at[from_slot, part], dst_ref=dst.at[far, place, part],
            send_sem=send.at[stage, step, peer[1]], recv_sem=recv.at[stage, step, order],
            device_id={"head": peer[0]}, device_id_type=MESH,
        )

    def q_copies(stage, step, peer, order):
        source = set_of(stages[stage][0], peer[0])
        return (
            row_copy(q_mine, q_all, q_send, q_recv, stage, step, peer, source, order),
            row_copy(do_mine, do_all, do_send, do_recv, stage, step, peer, source, order),
        )

    def dq_copy(stage, step, peer, order):
        far = stages[stage][0]
        return row_copy(dq_out.at[far], dq_in, dq_send, dq_recv, stage, step, peer, peer[1], order)

    def win_copy():
        return pltpu.make_async_remote_copy(
            src_ref=win_out, dst_ref=win_in, send_sem=win_sems.at[0], recv_sem=win_sems.at[1],
            device_id={"head": far_h}, device_id_type=MESH,
        )

    def far_copy(group):
        return pltpu.make_async_remote_copy(
            src_ref=kv_ref.at[group], dst_ref=kv_all.at[stage_of[1, group], me_s],
            send_sem=far_send.at[group], recv_sem=far_recv.at[group],
            device_id={"head": far_h}, device_id_type=MESH,
        )

    def plane_copy(stage, new, there):
        block = kv_all.at[stage, me_s, pl.ds(2 * new, 2)]
        return pltpu.make_async_remote_copy(
            src_ref=block, dst_ref=block,
            send_sem=plane_send.at[stage, new, there], recv_sem=kv_recv.at[stage, new, me_s],
            device_id={"seq": there * 2 + side}, device_id_type=MESH,
        )

    def sib_copy(stage, new, owner):
        block = kv_all.at[stage, owner, pl.ds(2 * new, 2)]
        return pltpu.make_async_remote_copy(
            src_ref=block, dst_ref=block,
            send_sem=sib_send.at[stage, new, owner // 2], recv_sem=kv_recv.at[stage, new, owner],
            device_id={"seq": sibling}, device_id_type=MESH,
        )

    def part_copy(stage, kind, there):
        return pltpu.make_async_remote_copy(
            src_ref=sib_out.at[stage, kind, there], dst_ref=sib_in.at[stage, kind, there],
            send_sem=part_send.at[stage, kind, there], recv_sem=part_recv.at[stage, kind, there],
            device_id={"seq": sibling}, device_id_type=MESH,
        )

    def term_copy(stage, kind, there, slot):
        far, group = stages[stage]
        dst, recv = (fold_in, fold_recv) if far else (term_in, term_recv)
        return pltpu.make_async_remote_copy(
            src_ref=chip_sum.at[stage, kind, there], dst_ref=dst.at[group, kind, slot],
            send_sem=term_send.at[stage, kind, there], recv_sem=recv.at[group, kind, slot],
            device_id={"seq": there * 2 + side}, device_id_type=MESH,
        )

    def back_copy(group, kind):
        return pltpu.make_async_remote_copy(
            src_ref=fold_out.at[group, kind], dst_ref=term_in.at[group, kind, chips],
            send_sem=back_send.at[group, kind], recv_sem=term_recv.at[group, kind, chips],
            device_id={"head": far_h}, device_id_type=MESH,
        )

    barrier = pltpu.get_barrier_semaphore()
    for k in range(1, heads):
        pl.semaphore_signal(barrier, inc=1, device_id={"head": lax.rem(me_h + k, heads)}, device_id_type=MESH)
    for k in range(1, chips):
        pl.semaphore_signal(barrier, inc=1, device_id={"seq": chip_at(k) * 2 + side}, device_id_type=MESH)
    pl.semaphore_signal(barrier, inc=1, device_id={"seq": sibling}, device_id_type=MESH)

    for ref, out in ((q_ref, q_mine), (do_ref, do_mine)):
        wide[...] = ref[...].astype(jnp.float32).reshape(rows * all_heads, width)
        for head in range(all_heads):
            out[head // mine, head % mine] = wide[pl.ds(head, rows, stride=all_heads)].astype(narrow)
    for group in range(groups):
        win_out[group] = jnp.full(win_out.shape[1:], win_ref[group], jnp.int32)
        for kind, ref in enumerate((ko_ref, vo_ref, kn_ref, vn_ref)):
            kv_ref[group, kind] = ref[:, group]
        kv_all[stage_of[0, group], me_s] = kv_ref[group]

    pl.semaphore_wait(barrier, heads - 1 + chips - 1 + 1)

    def share(stage):
        for new in range(2):
            @pl.loop(1, chips)
            def _(k):
                @pl.when((chip_at(k) >= chip) | (new == 0))
                def _():
                    plane_copy(stage, new, chip_at(k)).start()

            sib_copy(stage, new, me_s).start()

    def relay(stage):
        far_copy(stages[stage][1]).wait_recv()
        share(stage)

    def service(stage):
        @pl.loop(1, chips)
        def _(k):
            there = chip_at(k)
            owner = there * 2 + side
            for new in range(2):
                @pl.when((there <= chip) | (new == 0))
                def _():
                    sib_copy(stage, new, owner).wait_recv()
                    sib_copy(stage, new, owner).start()

    def settle(stage):
        @pl.loop(0, chips)
        def _(there):
            owner = there * 2 + 1 - side
            for new in range(2):
                @pl.when((there <= chip) | (new == 0))
                def _():
                    sib_copy(stage, new, owner).wait_recv()

    def send_rows(stage, begin=0, end=steps):
        @pl.loop(begin, end)
        def _(step):
            for peer in peers:
                for copy in q_copies(stage, step, peer, place):
                    copy.start()

    send_rows(0, 0, 1)
    far_copy(0).start()
    share(0)
    send_rows(0, 1)
    win_copy().start()
    for group in range(1, groups):
        far_copy(group).start()
    for stage in range(1, len(stages)):
        send_rows(stage)

    for far in range(2):
        q_all[far, place] = q_mine[set_of(far, me_h)]
        do_all[far, place] = do_mine[set_of(far, me_h)]

    old_rows = pl.multiple_of(total - first_token, run)
    base = lax.rem(off_ref[0] + first_token, total)

    def build(stage):
        for kind in range(2):
            @pl.loop(0, seqs)
            def _(owner):
                sums[kind, pl.ds(owner * tokens, tokens)] = kv_all[stage, owner, kind].astype(jnp.float32)

            sums[kind, total : total + tokens] = sums[kind, :tokens]

            @pl.loop(0, (old_rows + tokens - 1) // tokens)
            def _(block):
                start = lax.rem(base + block * tokens, total)
                line[kind, pl.ds(pl.multiple_of(block * tokens, tokens), tokens)] = sums[
                    kind, pl.ds(start, tokens)
                ].astype(narrow)

            @pl.loop(0, me_s + 1)
            def _(block):
                line[kind, pl.ds(pl.multiple_of(old_rows + block * tokens, run), tokens)] = kv_all[stage, block, 2 + kind]

        far, group = stages[stage]
        window = (win_in if far else win_out)[group, :1]
        position = lax.broadcasted_iota(jnp.int32, bias.shape, 0) - total
        token = lax.rem(lax.broadcasted_iota(jnp.int32, bias.shape, 1), run)
        bias[...] = jnp.where((position <= token) & (position > token - window), 0.0, -jnp.inf)
        keys_t[...] = line[0, :span].T
        sums[...] = jnp.zeros_like(sums)

    def attend(stage, step):
        far, group = stages[stage]
        first = group * per_group + step * hb
        for peer in peers:
            for copy in q_copies(stage, step, peer, peer[1]):
                copy.wait_recv()
        q = jnp.concatenate([q_all[far, :, first + h].reshape(run, width) for h in range(hb)], 0)
        do = jnp.concatenate([do_all[far, :, first + h].reshape(run, width) for h in range(hb)], 0)
        scores = dot(line[0, :span], q, NT) + jnp.concatenate([bias[...]] * (hb * run // bias.shape[1]), 1)
        top = jnp.max(scores, axis=0, keepdims=True)
        grown = jnp.exp2((scores - top) * (scale * math.log2(math.e)))
        inverse = 1.0 / jnp.sum(grown, axis=0, keepdims=True)
        weight_grad = dot(line[1, :span], do, NT)
        delta = jnp.sum(grown * weight_grad, axis=0, keepdims=True) * inverse
        weights = grown * inverse
        dscore = (weights * (weight_grad - delta)).astype(narrow)
        dqt = dot(keys_t[...], dscore, NN) * scale
        for h in range(0, hb, 2):
            piece = dqt[:, h * run : (h + 2) * run].T.astype(narrow).reshape(2, half, rows, width)
            for k in range(2):
                dq_out[far, :, first + h + k] = piece[k]
        for peer in peers:
            dq_copy(stage, step, peer, place).start()
        sums[0, :span] += dot(dscore, q, NN)
        sums[1, :span] += dot(weights.astype(narrow), do, NN)

    def put(stage, kind, there, seq_side, load):
        k_part = load(0) * scale
        v_part = load(1)

        @pl.when(seq_side == side)
        def _():
            own_part[kind, there, :, :width] = k_part
            own_part[kind, there, :, width:] = v_part

        @pl.when(seq_side != side)
        def _():
            sib_out[stage, kind, there, :, :width] = k_part.astype(narrow)
            sib_out[stage, kind, there, :, width:] = v_part.astype(narrow)
            part_copy(stage, kind, there).start()

    def split(stage):
        @pl.loop(0, 2 * chip + 2)
        def _(block):
            part = pl.ds(pl.multiple_of(old_rows + block * tokens, run), tokens)
            put(stage, 1, block // 2, lax.rem(block, 2), lambda i: sums[i, part])

        @pl.loop(old_rows // run, total // run)
        def _(block):
            for kind in range(2):
                sums[kind, pl.ds(pl.multiple_of(block * run, run), run)] = jnp.zeros((run, width), jnp.float32)

        for kind in range(2):
            sums[kind, total : total + tokens] = sums[kind, :tokens]

        @pl.loop(0, seqs)
        def _(block):
            start = lax.rem(block * tokens + total - base, total)
            put(stage, 0, block // 2, lax.rem(block, 2), lambda i: sums[i, pl.ds(start, tokens)])

    def finish(stage):
        for kind in range(2):
            @pl.loop(0, chips)
            def _(k):
                there = chip_at(k + 1)

                @pl.when((there <= chip) | (kind == 0))
                def _():
                    part_copy(stage, kind, there).wait_recv()
                    both = own_part[kind, there] + sib_in[stage, kind, there].astype(jnp.float32)
                    chip_sum[stage, kind, there] = both.astype(narrow)

                    @pl.when(there != chip)
                    def _():
                        term_copy(stage, kind, there, chip).start()

    def gather(stage, kind):
        far, group = stages[stage]
        source = fold_in if far else term_in
        own_part[kind, 0] = chip_sum[stage, kind, chip].astype(jnp.float32)

        @pl.loop(1, chips)
        def _(k):
            there = chip_at(k)

            @pl.when((there >= chip) | (kind == 0))
            def _():
                term_copy(stage, kind, there, there).wait_recv()
                own_part[kind, 0] += source[group, kind, there].astype(jnp.float32)

    def fold(stage):
        group = stages[stage][1]
        for kind in range(2):
            gather(stage, kind)
            fold_out[group, kind] = own_part[kind, 0].astype(narrow)
            back_copy(group, kind).start()

    last = len(stages) - 1
    relay(1)
    service(0)
    settle(0)
    win_copy().wait_recv()
    for stage in range(last + 1):
        build(stage)

        @pl.loop(0, steps)
        def _(step):
            @pl.when(step == steps - 1)
            def _():
                if stage == 0:
                    for later in range(2, groups + 1):
                        relay(later)
                    for later in range(groups + 1, last + 1):
                        share(later)
                if stage > 0:
                    finish(stage - 1)
                if stage == last:
                    for group in range(groups - 1):
                        fold(stage_of[1, group])
                if stage < last:
                    service(stage + 1)

            attend(stage, step)

        split(stage)
        if stage < last:
            settle(stage + 1)

    finish(last)
    fold(stage_of[1, groups - 1])

    for far in range(2):
        dq_ref[pl.ds(set_of(far, me_h) * mine, mine)] = dq_out[far, place]
        for peer in peers:
            for group in range(groups):
                @pl.loop(0, steps)
                def _(step):
                    dq_copy(stage_of[far, group], step, peer, peer[1]).wait_recv()

            dq_ref[pl.ds(set_of(far, peer[0]) * mine, mine)] = dq_in[far, peer[1]]

    for group in range(groups):
        for kind in range(2):
            gather(stage_of[0, group], kind)
            back_copy(group, kind).wait_recv()
            own_part[kind, 0] += term_in[group, kind, chips].astype(jnp.float32)
            for part in range(2):
                grad_ref[kind * 2 + part, pl.ds(group, tokens, stride=groups)] = own_part[
                    kind, 0, :, part * width : (part + 1) * width
                ]

    win_copy().wait_send()
    for group in range(groups):
        far_copy(group).wait_send()
        for kind in range(2):
            back_copy(group, kind).wait_send()
    for stage in range(last + 1):
        @pl.loop(0, steps)
        def _(step):
            for peer in peers:
                for copy in q_copies(stage, step, peer, place):
                    copy.wait_send()
                dq_copy(stage, step, peer, place).wait_send()

        for kind in range(2):
            sib_copy(stage, kind, me_s).wait_send()

            @pl.loop(1, chips)
            def _(k):
                there = chip_at(k)

                @pl.when((there >= chip) | (kind == 0))
                def _():
                    plane_copy(stage, kind, there).wait_send()

                @pl.when((there <= chip) | (kind == 0))
                def _():
                    sib_copy(stage, kind, there * 2 + side).wait_send()
                    term_copy(stage, kind, there, chip).wait_send()

            @pl.loop(0, chips)
            def _(there):
                @pl.when((there <= chip) | (kind == 0))
                def _():
                    part_copy(stage, kind, there).wait_send()


def plain_shards(query, key_new, value_new, key_old, value_old, offset, windows, grad_out):
    heads, seqs = lax.axis_size("head"), lax.axis_size("seq")
    rows, all_heads, width = query.shape
    tokens = rows * heads
    total = tokens * seqs
    groups = key_new.shape[1]
    span = total + tokens
    mine = all_heads // heads
    per_group = mine // groups
    hb = max(h for h in (1, 2, 4) if per_group % h == 0 and (h <= 1 or h * tokens * span <= 700_000))
    chunks = mine // hb

    def by_head(x):
        return x.transpose(1, 0, 2).reshape(heads, mine, rows, width)

    kv = [x.reshape(tokens, groups * width) for x in (key_old, value_old, key_new, value_new)]
    vmem = pl.BlockSpec(memory_space=pltpu.VMEM)
    smem = pl.BlockSpec(memory_space=pltpu.SMEM)
    narrow, wide = jnp.bfloat16, jnp.float32
    row_shape = (heads, mine, rows, width)
    row_sems = pltpu.SemaphoreType.DMA((chunks, heads))
    seq_sems = pltpu.SemaphoreType.DMA((seqs,))
    term_sems = pltpu.SemaphoreType.DMA((groups, seqs))
    term_shape = (groups, 2, seqs, tokens, 2 * width)
    dq, grads = pl.pallas_call(
        functools.partial(plain_kernel, heads, seqs, per_group, hb),
        in_specs=[smem, smem] + [vmem] * 6,
        out_specs=[vmem, vmem],
        out_shape=[
            jax.ShapeDtypeStruct((all_heads, rows, width), narrow),
            jax.ShapeDtypeStruct((groups, 2, tokens, 2 * width), wide),
        ],
        scratch_shapes=[
            pltpu.VMEM(row_shape, narrow),
            pltpu.VMEM(row_shape, narrow),
            pltpu.VMEM((seqs, 4, tokens, groups * width), narrow),
            pltpu.VMEM((2, span, groups * width), narrow),
            pltpu.VMEM((width, span), narrow),
            pltpu.VMEM((span, tokens), wide),
            pltpu.VMEM((span, 2 * width), wide),
            pltpu.VMEM((span, 2 * width), narrow),
            pltpu.VMEM(term_shape, narrow),
            pltpu.VMEM(term_shape, narrow),
            pltpu.VMEM(row_shape, narrow),
            pltpu.VMEM(row_shape, narrow),
            row_sems, row_sems, row_sems, row_sems, seq_sems, seq_sems, seq_sems,
            row_sems, row_sems, term_sems, term_sems, term_sems, term_sems,
        ],
        compiler_params=pltpu.CompilerParams(
            collective_id=0, has_side_effects=True, vmem_limit_bytes=62 * 2**20
        ),
    )(windows, offset, by_head(query), by_head(grad_out), *kv)
    grad_query = lax.optimization_barrier(dq.transpose(1, 0, 2)).astype(wide)
    grads = grads.reshape(groups, 2, tokens, 2, width).transpose(1, 3, 2, 0, 4)
    return (grad_query, grads[1, 0], grads[1, 1], grads[0, 0], grads[0, 1])


def shards(query, key_new, value_new, key_old, value_old, offset, windows, grad_out):
    heads, seqs = lax.axis_size("head"), lax.axis_size("seq")
    rows, all_heads, width = query.shape
    tokens = rows * heads
    total = tokens * seqs
    groups = key_new.shape[1]
    chips = seqs // 2
    half = heads // 2
    run = tokens // 2
    span = total + run
    padded = total + 2 * tokens
    mine = all_heads // heads
    per_group = mine // groups
    stages = 2 * groups
    budget = 60 * 2**20
    kept = total * width * (20 * stages + 8 * groups + 8) + 16 * padded * width + 20 * all_heads * rows * width
    fits = [h for h in (2, 4, 6) if per_group % h == 0 and 14 * h * run * span + kept < budget]
    if not fits or heads % 2 or seqs % 2:
        return plain_shards(query, key_new, value_new, key_old, value_old, offset, windows, grad_out)
    hb = max(fits)
    steps = per_group // hb

    vmem = pl.BlockSpec(memory_space=pltpu.VMEM)
    smem = pl.BlockSpec(memory_space=pltpu.SMEM)
    narrow, wide = jnp.bfloat16, jnp.float32
    row_shape = (heads, mine, rows, width)
    set_shape = (2, half, mine, rows, width)
    block = (tokens, 2 * width)
    dma = pltpu.SemaphoreType.DMA
    row_sems = dma((stages, steps, half))
    dq, grads = pl.pallas_call(
        functools.partial(kernel, heads, seqs, per_group, hb),
        in_specs=[smem, smem] + [vmem] * 6,
        out_specs=[vmem, vmem],
        out_shape=[
            jax.ShapeDtypeStruct((all_heads, rows, width), narrow),
            jax.ShapeDtypeStruct((4, tokens * groups, width), wide),
        ],
        scratch_shapes=[
            pltpu.VMEM((rows * all_heads, width), wide),
            pltpu.VMEM(row_shape, narrow),
            pltpu.VMEM(row_shape, narrow),
            pltpu.VMEM(set_shape, narrow),
            pltpu.VMEM(set_shape, narrow),
            pltpu.VMEM((stages, seqs, 4, tokens, width), narrow),
            pltpu.VMEM((2, padded, width), narrow),
            pltpu.VMEM((width, span), narrow),
            pltpu.VMEM((span, 2 * run), wide),
            pltpu.VMEM((2, padded, width), wide),
            pltpu.VMEM((groups, 8, 2 * run), jnp.int32),
            pltpu.VMEM((groups, 8, 2 * run), jnp.int32),
            pltpu.VMEM((groups, 4, tokens, width), narrow),
            pltpu.VMEM((2, chips) + block, wide),
            pltpu.VMEM((stages, 2, chips) + block, narrow),
            pltpu.VMEM((stages, 2, chips) + block, narrow),
            pltpu.VMEM((stages, 2, chips) + block, narrow),
            pltpu.VMEM((groups, 2, chips + 1) + block, narrow),
            pltpu.VMEM((groups, 2, chips) + block, narrow),
            pltpu.VMEM((groups, 2) + block, narrow),
            pltpu.VMEM(set_shape, narrow),
            pltpu.VMEM(set_shape, narrow),
            row_sems, row_sems, row_sems, row_sems, row_sems, row_sems, dma((2,)),
            dma((groups,)), dma((groups,)), dma((stages, 2, chips)), dma((stages, 2, chips)), dma((stages, 2, seqs)),
            dma((stages, 2, chips)), dma((stages, 2, chips)), dma((stages, 2, chips)),
            dma((groups, 2, chips + 1)), dma((groups, 2, chips)), dma((groups, 2)),
        ],
        compiler_params=pltpu.CompilerParams(
            collective_id=0, has_side_effects=True, vmem_limit_bytes=62 * 2**20
        ),
    )(windows, offset, query, grad_out, key_old, value_old, key_new, value_new)
    grad_query = lax.optimization_barrier(dq.transpose(1, 0, 2)).astype(wide)
    grads = grads.reshape(4, tokens, groups, width)
    return (grad_query, grads[2], grads[3], grads[0], grads[1])


def solution(mesh):
    tokens = P(("seq", "head"), None, None)
    slots = P("seq", "head", None)
    return jax.shard_map(
        shards,
        mesh=mesh,
        in_specs=(tokens, slots, slots, slots, slots, P(), P("head"), tokens),
        out_specs=(tokens, slots, slots, slots, slots),
        check_vma=False,
    )
```

```python
import functools
import math

import jax
import jax.numpy as jnp
from jax import lax
from jax.experimental import pallas as pl
from jax.experimental.pallas import tpu as pltpu
from jax.sharding import PartitionSpec as P

MESH = pl.DeviceIdType.MESH
NT = (((1,), (1,)), ((), ()))
NN = (((1,), (0,)), ((), ()))


def dot(a, b, dims):
    return lax.dot_general(a, b, dims, preferred_element_type=jnp.float32)


def plain_kernel(
    heads, seqs, per_group, heads_at_once,
    win_ref, off_ref, q_ref, do_ref, ko_ref, vo_ref, kn_ref, vn_ref,
    dq_ref, grad_ref,
    q_all, do_all, kv_all, line, keys_t, bias, sums, terms, term_out, term_in, dq_out, dq_in,
    q_send, q_recv, do_send, do_recv, kv_send, kv_recv, pass_send, dq_send, dq_recv, old_send, old_recv, new_send, new_recv,
):
    hb = heads_at_once
    me_h, me_s = lax.axis_index("head"), lax.axis_index("seq")
    rows, width = q_ref.shape[2:]
    tokens = rows * heads
    groups = q_ref.shape[1] // per_group
    total = tokens * seqs
    span = total + tokens
    steps = per_group // hb
    chunks = groups * steps
    scale = 1.0 / math.sqrt(width)

    def peer_h(k):
        return lax.rem(me_h + k, heads)

    def peer_s(k):
        return lax.rem(me_s + k, seqs)

    def row_copy(src, dst, send, recv, chunk, there, slot):
        part = pl.ds(chunk * hb, hb)
        return pltpu.make_async_remote_copy(
            src_ref=src.at[there, part], dst_ref=dst.at[slot, part],
            send_sem=send.at[chunk, there], recv_sem=recv.at[chunk, slot],
            device_id={"head": there}, device_id_type=MESH,
        )

    def kv_copy(there, slot):
        return pltpu.make_async_remote_copy(
            src_ref=kv_all.at[me_s], dst_ref=kv_all.at[slot],
            send_sem=kv_send.at[there], recv_sem=kv_recv.at[slot],
            device_id={"seq": there}, device_id_type=MESH,
        )

    partner = me_s + 1 - 2 * lax.rem(me_s, 2)

    def pass_copy(slot):
        return pltpu.make_async_remote_copy(
            src_ref=kv_all.at[slot], dst_ref=kv_all.at[slot],
            send_sem=pass_send.at[slot], recv_sem=kv_recv.at[slot],
            device_id={"seq": partner}, device_id_type=MESH,
        )

    def term_copy(group, kind, there, slot):
        send, recv = ((old_send, old_recv), (new_send, new_recv))[kind]
        return pltpu.make_async_remote_copy(
            src_ref=term_out.at[group, kind, there], dst_ref=term_in.at[group, kind, slot],
            send_sem=send.at[group, there], recv_sem=recv.at[group, slot],
            device_id={"seq": there}, device_id_type=MESH,
        )

    for kind, ref in enumerate((ko_ref, vo_ref, kn_ref, vn_ref)):
        kv_all[me_s, kind] = ref[...]

    barrier = pltpu.get_barrier_semaphore()
    for k in range(1, heads):
        pl.semaphore_signal(barrier, inc=1, device_id={"head": peer_h(k)}, device_id_type=MESH)
    for k in range(1, seqs):
        pl.semaphore_signal(barrier, inc=1, device_id={"seq": peer_s(k)}, device_id_type=MESH)
    pl.semaphore_wait(barrier, heads + seqs - 2)

    @pl.loop(1, seqs // 2)
    def _(k):
        kv_copy(peer_s(2 * k), me_s).start()

    kv_copy(partner, me_s).start()

    @pl.loop(0, chunks)
    def _(chunk):
        for k in range(1, heads):
            row_copy(q_ref, q_all, q_send, q_recv, chunk, peer_h(k), me_h).start()
            row_copy(do_ref, do_all, do_send, do_recv, chunk, peer_h(k), me_h).start()

    q_all[me_h] = q_ref[me_h]
    do_all[me_h] = do_ref[me_h]

    @pl.loop(1, seqs // 2)
    def _(k):
        slot = peer_s(2 * k)
        kv_copy(slot, slot).wait_recv()
        pass_copy(slot).start()

    @pl.loop(0, seqs // 2)
    def _(k):
        slot = lax.rem(partner + 2 * k, seqs)
        kv_copy(slot, slot).wait_recv()

    base = lax.rem(off_ref[0] + me_s * tokens, total)
    old_rows = total - me_s * tokens

    def slot_of(row):
        slot = row + base
        return jnp.where(slot >= total, slot - total, slot)

    @pl.loop(0, seqs - me_s)
    def _(block):
        row = block * tokens + lax.broadcasted_iota(jnp.int32, (tokens, total), 0)
        slot = lax.broadcasted_iota(jnp.int32, (tokens, total), 1)
        pick = jnp.where(slot_of(row) == slot, 1.0, 0.0).astype(jnp.bfloat16)
        for kind in range(2):
            stored = kv_all[:, kind].reshape(total, groups * width)
            line[kind, pl.ds(block * tokens, tokens)] = dot(pick, stored, NN).astype(jnp.bfloat16)

    @pl.loop(0, me_s + 1)
    def _(block):
        for kind in range(2):
            line[kind, pl.ds((seqs - me_s + block) * tokens, tokens)] = kv_all[block, 2 + kind]

    for group in range(groups):
        left = group * width
        window = win_ref[group]
        place = lax.broadcasted_iota(jnp.int32, (span, tokens), 0) - total
        token = lax.broadcasted_iota(jnp.int32, (span, tokens), 1)
        bias[...] = jnp.where((place <= token) & (place > token - window), 0.0, -jnp.inf)
        keys_t[...] = line[0, :, left : left + width].T
        sums[...] = jnp.zeros_like(sums)

        @pl.loop(0, steps)
        def _(step):
            chunk = group * steps + step
            first = chunk * hb
            for k in range(1, heads):
                row_copy(q_ref, q_all, q_send, q_recv, chunk, peer_h(k), peer_h(k)).wait_recv()
                row_copy(do_ref, do_all, do_send, do_recv, chunk, peer_h(k), peer_h(k)).wait_recv()
            q = jnp.concatenate([q_all[:, first + h].reshape(tokens, width) for h in range(hb)], 0)
            do = jnp.concatenate([do_all[:, first + h].reshape(tokens, width) for h in range(hb)], 0)
            keys = line[0, :, left : left + width]
            values = line[1, :, left : left + width]
            scores = dot(keys, q, NT) + jnp.concatenate([bias[...]] * hb, 1)
            top = jnp.max(scores, axis=0, keepdims=True)
            grown = jnp.exp2((scores - top) * (scale * math.log2(math.e)))
            inverse = 1.0 / jnp.sum(grown, axis=0, keepdims=True)
            weight_grad = dot(values, do, NT)
            delta = jnp.sum(grown * weight_grad, axis=0, keepdims=True) * inverse
            weights = grown * inverse
            dscore = (weights * (weight_grad - delta)).astype(jnp.bfloat16)
            dqt = dot(keys_t[...], dscore, NN) * scale
            for h in range(hb):
                piece = dqt[:, h * tokens : (h + 1) * tokens].T.astype(jnp.bfloat16)
                dq_out[:, first + h] = piece.reshape(heads, rows, width)
            for k in range(1, heads):
                row_copy(dq_out, dq_in, dq_send, dq_recv, chunk, peer_h(k), me_h).start()
            sums[:, :width] += dot(dscore, q, NN)
            sums[:, width:] += dot(weights.astype(jnp.bfloat16), do, NN)

        terms[:, :width] = (sums[:, :width] * scale).astype(jnp.bfloat16)
        terms[:, width:] = sums[:, width:].astype(jnp.bfloat16)

        @pl.loop(0, seqs)
        def _(k):
            there = peer_s(k)
            row = lax.broadcasted_iota(jnp.int32, (tokens, total), 1)
            slot = there * tokens + lax.broadcasted_iota(jnp.int32, (tokens, total), 0)
            chosen = (slot_of(row) == slot) & (row < old_rows)
            pick = jnp.where(chosen, 1.0, 0.0).astype(jnp.bfloat16)
            term_out[group, 0, there] = dot(pick, terms[:total], NN).astype(jnp.bfloat16)

            @pl.when(there <= me_s)
            def _():
                term_out[group, 1, there] = terms[pl.ds((seqs - me_s + there) * tokens, tokens)]

            @pl.when(k > 0)
            def _():
                term_copy(group, 0, there, me_s).start()

                @pl.when(there < me_s)
                def _():
                    term_copy(group, 1, there, me_s).start()

    for k in range(heads):
        there = peer_h(k)
        place = pl.ds(there * groups * per_group, groups * per_group)
        if k == 0:
            dq_ref[place] = dq_out[there]
            continue

        @pl.loop(0, chunks)
        def _(chunk):
            row_copy(dq_out, dq_in, dq_send, dq_recv, chunk, there, there).wait_recv()

        dq_ref[place] = dq_in[there]

    for group in range(groups):
        for kind in range(2):
            grad_ref[group, kind] = term_out[group, kind, me_s].astype(jnp.float32)

        @pl.loop(1, seqs)
        def _(k):
            there = peer_s(k)
            term_copy(group, 0, there, there).wait_recv()
            grad_ref[group, 0] += term_in[group, 0, there].astype(jnp.float32)

            @pl.when(there > me_s)
            def _():
                term_copy(group, 1, there, there).wait_recv()
                grad_ref[group, 1] += term_in[group, 1, there].astype(jnp.float32)

    kv_copy(partner, me_s).wait_send()

    @pl.loop(1, seqs // 2)
    def _(k):
        kv_copy(peer_s(2 * k), me_s).wait_send()
        pass_copy(peer_s(2 * k)).wait_send()

    @pl.loop(0, chunks)
    def _(chunk):
        for k in range(1, heads):
            row_copy(q_ref, q_all, q_send, q_recv, chunk, peer_h(k), me_h).wait_send()
            row_copy(do_ref, do_all, do_send, do_recv, chunk, peer_h(k), me_h).wait_send()
            row_copy(dq_out, dq_in, dq_send, dq_recv, chunk, peer_h(k), me_h).wait_send()

    @pl.loop(1, seqs)
    def _(k):
        there = peer_s(k)
        for group in range(groups):
            term_copy(group, 0, there, me_s).wait_send()

            @pl.when(there < me_s)
            def _():
                term_copy(group, 1, there, me_s).wait_send()


def kernel(
    heads, seqs, per_group, heads_at_once,
    win_ref, off_ref, q_ref, do_ref, ko_ref, vo_ref, kn_ref, vn_ref,
    dq_ref, grad_ref,
    wide, q_mine, do_mine, q_all, do_all, kv_all, line, keys_t, bias, sums, win_out, win_in, kv_ref,
    own_part, sib_out, sib_in, chip_sum, term_in, fold_in, fold_out, dq_out, dq_in,
    q_send, q_recv, do_send, do_recv, dq_send, dq_recv, win_sems,
    far_send, far_recv, plane_send, sib_send, kv_recv,
    part_send, part_recv, term_send, term_recv, fold_recv, back_send,
):
    hb = heads_at_once
    half = heads // 2
    chips = seqs // 2
    me_h, me_s = lax.axis_index("head"), lax.axis_index("seq")
    chip, side = me_s // 2, lax.rem(me_s, 2)
    sibling = chip * 2 + 1 - side
    pair, place = me_h // half, lax.rem(me_h, half)
    far_h = lax.rem(me_h + half, heads)
    rows, all_heads, width = q_ref.shape
    mine = all_heads // heads
    groups = mine // per_group
    tokens = rows * heads
    run = rows * half
    total = tokens * seqs
    span = total + run
    steps = per_group // hb
    scale = 1.0 / math.sqrt(width)
    first_token = me_s * tokens + pair * run
    narrow = jnp.bfloat16

    stages = [(0, 0)] + [(1, g) for g in range(groups)] + [(0, g) for g in range(1, groups)]
    stage_of = {key: at for at, key in enumerate(stages)}
    peers = []
    for dj in range(1, half):
        there = lax.rem(place + dj, half)
        peers.append((pair * half + there, there))

    def set_of(far, head):
        return lax.rem(head + half, heads) if far else head

    def chip_at(k):
        return lax.rem(chip + k, chips)

    def row_copy(src, dst, send, recv, stage, step, peer, from_slot, order):
        far, group = stages[stage]
        part = pl.ds(group * per_group + step * hb, hb)
        return pltpu.make_async_remote_copy(
            src_ref=src.at[from_slot, part], dst_ref=dst.at[far, place, part],
            send_sem=send.at[stage, step, peer[1]], recv_sem=recv.at[stage, step, order],
            device_id={"head": peer[0]}, device_id_type=MESH,
        )

    def q_copies(stage, step, peer, order):
        source = set_of(stages[stage][0], peer[0])
        return (
            row_copy(q_mine, q_all, q_send, q_recv, stage, step, peer, source, order),
            row_copy(do_mine, do_all, do_send, do_recv, stage, step, peer, source, order),
        )

    def dq_copy(stage, step, peer, order):
        far = stages[stage][0]
        return row_copy(dq_out.at[far], dq_in, dq_send, dq_recv, stage, step, peer, peer[1], order)

    def win_copy():
        return pltpu.make_async_remote_copy(
            src_ref=win_out, dst_ref=win_in, send_sem=win_sems.at[0], recv_sem=win_sems.at[1],
            device_id={"head": far_h}, device_id_type=MESH,
        )

    def far_copy(group, new):
        part = pl.ds(2 * new, 2)
        return pltpu.make_async_remote_copy(
            src_ref=kv_ref.at[group, part], dst_ref=kv_all.at[stage_of[1, group], me_s, part],
            send_sem=far_send.at[group, new], recv_sem=far_recv.at[group, new],
            device_id={"head": far_h}, device_id_type=MESH,
        )

    def plane_copy(stage, new, there):
        block = kv_all.at[stage, me_s, pl.ds(2 * new, 2)]
        return pltpu.make_async_remote_copy(
            src_ref=block, dst_ref=block,
            send_sem=plane_send.at[stage, new, there], recv_sem=kv_recv.at[stage, new, me_s],
            device_id={"seq": there * 2 + side}, device_id_type=MESH,
        )

    def sib_copy(stage, new, owner):
        block = kv_all.at[stage, owner, pl.ds(2 * new, 2)]
        return pltpu.make_async_remote_copy(
            src_ref=block, dst_ref=block,
            send_sem=sib_send.at[stage, new, owner // 2], recv_sem=kv_recv.at[stage, new, owner],
            device_id={"seq": sibling}, device_id_type=MESH,
        )

    def part_copy(stage, kind, there):
        return pltpu.make_async_remote_copy(
            src_ref=sib_out.at[stage, kind, there], dst_ref=sib_in.at[stage, kind, there],
            send_sem=part_send.at[stage, kind, there], recv_sem=part_recv.at[stage, kind, there],
            device_id={"seq": sibling}, device_id_type=MESH,
        )

    def term_copy(stage, kind, there, slot):
        far, group = stages[stage]
        dst, recv = (fold_in, fold_recv) if far else (term_in, term_recv)
        return pltpu.make_async_remote_copy(
            src_ref=chip_sum.at[stage, kind, there], dst_ref=dst.at[group, kind, slot],
            send_sem=term_send.at[stage, kind, there], recv_sem=recv.at[group, kind, slot],
            device_id={"seq": there * 2 + side}, device_id_type=MESH,
        )

    def back_copy(group, kind):
        return pltpu.make_async_remote_copy(
            src_ref=fold_out.at[group, kind], dst_ref=term_in.at[group, kind, chips],
            send_sem=back_send.at[group, kind], recv_sem=term_recv.at[group, kind, chips],
            device_id={"head": far_h}, device_id_type=MESH,
        )

    barrier = pltpu.get_barrier_semaphore()
    for there in [far_h] + [peer[0] for peer in peers]:
        pl.semaphore_signal(barrier, inc=1, device_id={"head": there}, device_id_type=MESH)
    for k in range(1, chips):
        pl.semaphore_signal(barrier, inc=1, device_id={"seq": chip_at(k) * 2 + side}, device_id_type=MESH)
    pl.semaphore_signal(barrier, inc=1, device_id={"seq": sibling}, device_id_type=MESH)

    for group in range(groups):
        win_out[group] = jnp.full(win_out.shape[1:], win_ref[group], jnp.int32)
        for kind, ref in enumerate((ko_ref, vo_ref, kn_ref, vn_ref)):
            kv_ref[group, kind] = ref[:, group]
        kv_all[stage_of[0, group], me_s] = kv_ref[group]

    pl.semaphore_wait(barrier, 1 + len(peers) + chips - 1 + 1)

    def share(stage, parts=(0, 1)):
        for new in parts:
            @pl.loop(1, chips)
            def _(k):
                @pl.when((chip_at(k) >= chip) | (new == 0))
                def _():
                    plane_copy(stage, new, chip_at(k)).start()

            sib_copy(stage, new, me_s).start()

    def relay(stage):
        for new in range(2):
            far_copy(stages[stage][1], new).wait_recv()
            share(stage, (new,))

    def service(stage):
        @pl.loop(1, chips)
        def _(k):
            there = chip_at(k)
            owner = there * 2 + side
            for new in range(2):
                @pl.when((there <= chip) | (new == 0))
                def _():
                    sib_copy(stage, new, owner).wait_recv()
                    sib_copy(stage, new, owner).start()

    def settle(stage):
        @pl.loop(0, chips)
        def _(there):
            owner = there * 2 + 1 - side
            for new in range(2):
                @pl.when((there <= chip) | (new == 0))
                def _():
                    sib_copy(stage, new, owner).wait_recv()

    def send_rows(stage, begin=0, end=steps):
        @pl.loop(begin, end)
        def _(step):
            for peer in peers:
                for copy in q_copies(stage, step, peer, place):
                    copy.start()

    for new in range(2):
        far_copy(0, new).start()
    share(0)
    for ref, out in ((q_ref, q_mine), (do_ref, do_mine)):
        wide[...] = ref[...].astype(jnp.float32).reshape(rows * all_heads, width)
        for head in range(all_heads):
            out[head // mine, head % mine] = wide[pl.ds(head, rows, stride=all_heads)].astype(narrow)
    send_rows(0)
    win_copy().start()
    for group in range(1, groups):
        for new in range(2):
            far_copy(group, new).start()
    for stage in range(1, len(stages)):
        send_rows(stage)

    for far in range(2):
        q_all[far, place] = q_mine[set_of(far, me_h)]
        do_all[far, place] = do_mine[set_of(far, me_h)]

    old_rows = pl.multiple_of(total - first_token, run)
    base = lax.rem(off_ref[0] + first_token, total)

    def build(stage):
        for kind in range(2):
            @pl.loop(0, seqs)
            def _(owner):
                sums[kind, pl.ds(owner * tokens, tokens)] = kv_all[stage, owner, kind].astype(jnp.float32)

            sums[kind, total : total + tokens] = sums[kind, :tokens]

            @pl.loop(0, (old_rows + tokens - 1) // tokens)
            def _(block):
                start = lax.rem(base + block * tokens, total)
                line[kind, pl.ds(pl.multiple_of(block * tokens, tokens), tokens)] = sums[
                    kind, pl.ds(start, tokens)
                ].astype(narrow)

            @pl.loop(0, me_s + 1)
            def _(block):
                line[kind, pl.ds(pl.multiple_of(old_rows + block * tokens, run), tokens)] = kv_all[stage, block, 2 + kind]

        far, group = stages[stage]
        window = (win_in if far else win_out)[group, :1]
        position = lax.broadcasted_iota(jnp.int32, bias.shape, 0) - total
        token = lax.rem(lax.broadcasted_iota(jnp.int32, bias.shape, 1), run)
        bias[...] = jnp.where((position <= token) & (position > token - window), 0.0, -jnp.inf)
        keys_t[...] = line[0, :span].T
        sums[...] = jnp.zeros_like(sums)

    def attend(stage, step):
        far, group = stages[stage]
        first = group * per_group + step * hb
        for peer in peers:
            for copy in q_copies(stage, step, peer, peer[1]):
                copy.wait_recv()
        q = jnp.concatenate([q_all[far, :, first + h].reshape(run, width) for h in range(hb)], 0)
        do = jnp.concatenate([do_all[far, :, first + h].reshape(run, width) for h in range(hb)], 0)
        scores = dot(line[0, :span], q, NT) + jnp.concatenate([bias[...]] * (hb * run // bias.shape[1]), 1)
        top = jnp.max(scores, axis=0, keepdims=True)
        grown = jnp.exp2((scores - top) * (scale * math.log2(math.e)))
        inverse = 1.0 / jnp.sum(grown, axis=0, keepdims=True)
        weight_grad = dot(line[1, :span], do, NT)
        delta = jnp.sum(grown * weight_grad, axis=0, keepdims=True) * inverse
        weights = grown * inverse
        dscore = (weights * (weight_grad - delta)).astype(narrow)
        dqt = dot(keys_t[...], dscore, NN) * scale
        for h in range(0, hb, 2):
            piece = dqt[:, h * run : (h + 2) * run].T.astype(narrow).reshape(2, half, rows, width)
            for k in range(2):
                dq_out[far, :, first + h + k] = piece[k]
        for peer in peers:
            dq_copy(stage, step, peer, place).start()
        sums[0, :span] += dot(dscore, q, NN)
        sums[1, :span] += dot(weights.astype(narrow), do, NN)

    def put(stage, kind, there, seq_side, load):
        k_part = load(0) * scale
        v_part = load(1)

        @pl.when(seq_side == side)
        def _():
            own_part[kind, there, :, :width] = k_part
            own_part[kind, there, :, width:] = v_part

        @pl.when(seq_side != side)
        def _():
            sib_out[stage, kind, there, :, :width] = k_part.astype(narrow)
            sib_out[stage, kind, there, :, width:] = v_part.astype(narrow)
            part_copy(stage, kind, there).start()

    def split(stage):
        @pl.loop(0, 2 * chip + 2)
        def _(block):
            part = pl.ds(pl.multiple_of(old_rows + block * tokens, run), tokens)
            put(stage, 1, block // 2, lax.rem(block, 2), lambda i: sums[i, part])

        @pl.loop(old_rows // run, total // run)
        def _(block):
            for kind in range(2):
                sums[kind, pl.ds(pl.multiple_of(block * run, run), run)] = jnp.zeros((run, width), jnp.float32)

        for kind in range(2):
            sums[kind, total : total + tokens] = sums[kind, :tokens]

        @pl.loop(0, seqs)
        def _(block):
            start = lax.rem(block * tokens + total - base, total)
            put(stage, 0, block // 2, lax.rem(block, 2), lambda i: sums[i, pl.ds(start, tokens)])

    def finish(stage):
        for kind in range(2):
            @pl.loop(0, chips)
            def _(k):
                there = chip_at(k + 1)

                @pl.when((there <= chip) | (kind == 0))
                def _():
                    part_copy(stage, kind, there).wait_recv()
                    both = own_part[kind, there] + sib_in[stage, kind, there].astype(jnp.float32)
                    chip_sum[stage, kind, there] = both.astype(narrow)

                    @pl.when(there != chip)
                    def _():
                        term_copy(stage, kind, there, chip).start()

    def gather(stage, kind):
        far, group = stages[stage]
        source = fold_in if far else term_in
        own_part[kind, 0] = chip_sum[stage, kind, chip].astype(jnp.float32)

        @pl.loop(1, chips)
        def _(k):
            there = chip_at(k)

            @pl.when((there >= chip) | (kind == 0))
            def _():
                term_copy(stage, kind, there, there).wait_recv()
                own_part[kind, 0] += source[group, kind, there].astype(jnp.float32)

    def fold(stage):
        group = stages[stage][1]
        for kind in range(2):
            gather(stage, kind)
            fold_out[group, kind] = own_part[kind, 0].astype(narrow)
            back_copy(group, kind).start()

    last = len(stages) - 1
    relay(1)
    service(0)
    settle(0)
    win_copy().wait_recv()
    for stage in range(last + 1):
        build(stage)

        @pl.loop(0, steps)
        def _(step):
            @pl.when(step == steps - 1)
            def _():
                if stage == 0:
                    for later in range(2, groups + 1):
                        relay(later)
                    for later in range(groups + 1, last + 1):
                        share(later)
                if stage > 0:
                    finish(stage - 1)
                if stage == last:
                    for group in range(groups - 1):
                        fold(stage_of[1, group])
                if stage < last:
                    service(stage + 1)

            attend(stage, step)

        split(stage)
        if stage < last:
            settle(stage + 1)

    finish(last)
    fold(stage_of[1, groups - 1])

    for far in range(2):
        dq_ref[pl.ds(set_of(far, me_h) * mine, mine)] = dq_out[far, place]
        for peer in peers:
            for group in range(groups):
                @pl.loop(0, steps)
                def _(step):
                    dq_copy(stage_of[far, group], step, peer, peer[1]).wait_recv()

            dq_ref[pl.ds(set_of(far, peer[0]) * mine, mine)] = dq_in[far, peer[1]]

    for group in range(groups):
        for kind in range(2):
            gather(stage_of[0, group], kind)
            back_copy(group, kind).wait_recv()
            own_part[kind, 0] += term_in[group, kind, chips].astype(jnp.float32)
            for part in range(2):
                grad_ref[kind * 2 + part, pl.ds(group, tokens, stride=groups)] = own_part[
                    kind, 0, :, part * width : (part + 1) * width
                ]

    win_copy().wait_send()
    for group in range(groups):
        for new in range(2):
            far_copy(group, new).wait_send()
        for kind in range(2):
            back_copy(group, kind).wait_send()
    for stage in range(last + 1):
        @pl.loop(0, steps)
        def _(step):
            for peer in peers:
                for copy in q_copies(stage, step, peer, place):
                    copy.wait_send()
                dq_copy(stage, step, peer, place).wait_send()

        for kind in range(2):
            sib_copy(stage, kind, me_s).wait_send()

            @pl.loop(1, chips)
            def _(k):
                there = chip_at(k)

                @pl.when((there >= chip) | (kind == 0))
                def _():
                    plane_copy(stage, kind, there).wait_send()

                @pl.when((there <= chip) | (kind == 0))
                def _():
                    sib_copy(stage, kind, there * 2 + side).wait_send()
                    term_copy(stage, kind, there, chip).wait_send()

            @pl.loop(0, chips)
            def _(there):
                @pl.when((there <= chip) | (kind == 0))
                def _():
                    part_copy(stage, kind, there).wait_send()


def plain_shards(query, key_new, value_new, key_old, value_old, offset, windows, grad_out):
    heads, seqs = lax.axis_size("head"), lax.axis_size("seq")
    rows, all_heads, width = query.shape
    tokens = rows * heads
    total = tokens * seqs
    groups = key_new.shape[1]
    span = total + tokens
    mine = all_heads // heads
    per_group = mine // groups
    hb = max(h for h in (1, 2, 4) if per_group % h == 0 and (h <= 1 or h * tokens * span <= 700_000))
    chunks = mine // hb

    def by_head(x):
        return x.transpose(1, 0, 2).reshape(heads, mine, rows, width)

    kv = [x.reshape(tokens, groups * width) for x in (key_old, value_old, key_new, value_new)]
    vmem = pl.BlockSpec(memory_space=pltpu.VMEM)
    smem = pl.BlockSpec(memory_space=pltpu.SMEM)
    narrow, wide = jnp.bfloat16, jnp.float32
    row_shape = (heads, mine, rows, width)
    row_sems = pltpu.SemaphoreType.DMA((chunks, heads))
    seq_sems = pltpu.SemaphoreType.DMA((seqs,))
    term_sems = pltpu.SemaphoreType.DMA((groups, seqs))
    term_shape = (groups, 2, seqs, tokens, 2 * width)
    dq, grads = pl.pallas_call(
        functools.partial(plain_kernel, heads, seqs, per_group, hb),
        in_specs=[smem, smem] + [vmem] * 6,
        out_specs=[vmem, vmem],
        out_shape=[
            jax.ShapeDtypeStruct((all_heads, rows, width), narrow),
            jax.ShapeDtypeStruct((groups, 2, tokens, 2 * width), wide),
        ],
        scratch_shapes=[
            pltpu.VMEM(row_shape, narrow),
            pltpu.VMEM(row_shape, narrow),
            pltpu.VMEM((seqs, 4, tokens, groups * width), narrow),
            pltpu.VMEM((2, span, groups * width), narrow),
            pltpu.VMEM((width, span), narrow),
            pltpu.VMEM((span, tokens), wide),
            pltpu.VMEM((span, 2 * width), wide),
            pltpu.VMEM((span, 2 * width), narrow),
            pltpu.VMEM(term_shape, narrow),
            pltpu.VMEM(term_shape, narrow),
            pltpu.VMEM(row_shape, narrow),
            pltpu.VMEM(row_shape, narrow),
            row_sems, row_sems, row_sems, row_sems, seq_sems, seq_sems, seq_sems,
            row_sems, row_sems, term_sems, term_sems, term_sems, term_sems,
        ],
        compiler_params=pltpu.CompilerParams(
            collective_id=0, has_side_effects=True, vmem_limit_bytes=62 * 2**20
        ),
    )(windows, offset, by_head(query), by_head(grad_out), *kv)
    grad_query = lax.optimization_barrier(dq.transpose(1, 0, 2)).astype(wide)
    grads = grads.reshape(groups, 2, tokens, 2, width).transpose(1, 3, 2, 0, 4)
    return (grad_query, grads[1, 0], grads[1, 1], grads[0, 0], grads[0, 1])


def shards(query, key_new, value_new, key_old, value_old, offset, windows, grad_out):
    heads, seqs = lax.axis_size("head"), lax.axis_size("seq")
    rows, all_heads, width = query.shape
    tokens = rows * heads
    total = tokens * seqs
    groups = key_new.shape[1]
    chips = seqs // 2
    half = heads // 2
    run = tokens // 2
    span = total + run
    padded = total + 2 * tokens
    mine = all_heads // heads
    per_group = mine // groups
    stages = 2 * groups
    budget = 60 * 2**20
    kept = total * width * (20 * stages + 8 * groups + 8) + 16 * padded * width + 20 * all_heads * rows * width
    fits = [h for h in (2, 4, 6) if per_group % h == 0 and 14 * h * run * span + kept < budget]
    if not fits or heads % 2 or seqs % 2:
        return plain_shards(query, key_new, value_new, key_old, value_old, offset, windows, grad_out)
    hb = max(fits)
    steps = per_group // hb

    vmem = pl.BlockSpec(memory_space=pltpu.VMEM)
    smem = pl.BlockSpec(memory_space=pltpu.SMEM)
    narrow, wide = jnp.bfloat16, jnp.float32
    row_shape = (heads, mine, rows, width)
    set_shape = (2, half, mine, rows, width)
    block = (tokens, 2 * width)
    dma = pltpu.SemaphoreType.DMA
    row_sems = dma((stages, steps, half))
    dq, grads = pl.pallas_call(
        functools.partial(kernel, heads, seqs, per_group, hb),
        in_specs=[smem, smem] + [vmem] * 6,
        out_specs=[vmem, vmem],
        out_shape=[
            jax.ShapeDtypeStruct((all_heads, rows, width), narrow),
            jax.ShapeDtypeStruct((4, tokens * groups, width), wide),
        ],
        scratch_shapes=[
            pltpu.VMEM((rows * all_heads, width), wide),
            pltpu.VMEM(row_shape, narrow),
            pltpu.VMEM(row_shape, narrow),
            pltpu.VMEM(set_shape, narrow),
            pltpu.VMEM(set_shape, narrow),
            pltpu.VMEM((stages, seqs, 4, tokens, width), narrow),
            pltpu.VMEM((2, padded, width), narrow),
            pltpu.VMEM((width, span), narrow),
            pltpu.VMEM((span, 2 * run), wide),
            pltpu.VMEM((2, padded, width), wide),
            pltpu.VMEM((groups, 8, 2 * run), jnp.int32),
            pltpu.VMEM((groups, 8, 2 * run), jnp.int32),
            pltpu.VMEM((groups, 4, tokens, width), narrow),
            pltpu.VMEM((2, chips) + block, wide),
            pltpu.VMEM((stages, 2, chips) + block, narrow),
            pltpu.VMEM((stages, 2, chips) + block, narrow),
            pltpu.VMEM((stages, 2, chips) + block, narrow),
            pltpu.VMEM((groups, 2, chips + 1) + block, narrow),
            pltpu.VMEM((groups, 2, chips) + block, narrow),
            pltpu.VMEM((groups, 2) + block, narrow),
            pltpu.VMEM(set_shape, narrow),
            pltpu.VMEM(set_shape, narrow),
            row_sems, row_sems, row_sems, row_sems, row_sems, row_sems, dma((2,)),
            dma((groups, 2)), dma((groups, 2)), dma((stages, 2, chips)), dma((stages, 2, chips)), dma((stages, 2, seqs)),
            dma((stages, 2, chips)), dma((stages, 2, chips)), dma((stages, 2, chips)),
            dma((groups, 2, chips + 1)), dma((groups, 2, chips)), dma((groups, 2)),
        ],
        compiler_params=pltpu.CompilerParams(
            collective_id=0, has_side_effects=True, vmem_limit_bytes=62 * 2**20
        ),
    )(windows, offset, query, grad_out, key_old, value_old, key_new, value_new)
    grad_query = lax.optimization_barrier(dq.transpose(1, 0, 2)).astype(wide)
    grads = grads.reshape(4, tokens, groups, width)
    return (grad_query, grads[2], grads[3], grads[0], grads[1])


def solution(mesh):
    tokens = P(("seq", "head"), None, None)
    slots = P("seq", "head", None)
    return jax.shard_map(
        shards,
        mesh=mesh,
        in_specs=(tokens, slots, slots, slots, slots, P(), P("head"), tokens),
        out_specs=(tokens, slots, slots, slots, slots),
        check_vma=False,
    )
```

```python
import functools
import math

import jax
import jax.numpy as jnp
from jax import lax
from jax.experimental import pallas as pl
from jax.experimental.pallas import tpu as pltpu
from jax.sharding import PartitionSpec as P

MESH = pl.DeviceIdType.MESH
NT = (((1,), (1,)), ((), ()))
NN = (((1,), (0,)), ((), ()))


def dot(a, b, dims):
    return lax.dot_general(a, b, dims, preferred_element_type=jnp.float32)


def plain_kernel(
    heads, seqs, per_group, heads_at_once,
    win_ref, off_ref, q_ref, do_ref, ko_ref, vo_ref, kn_ref, vn_ref,
    dq_ref, grad_ref,
    q_all, do_all, kv_all, line, keys_t, bias, sums, terms, term_out, term_in, dq_out, dq_in,
    q_send, q_recv, do_send, do_recv, kv_send, kv_recv, pass_send, dq_send, dq_recv, old_send, old_recv, new_send, new_recv,
):
    hb = heads_at_once
    me_h, me_s = lax.axis_index("head"), lax.axis_index("seq")
    rows, width = q_ref.shape[2:]
    tokens = rows * heads
    groups = q_ref.shape[1] // per_group
    total = tokens * seqs
    span = total + tokens
    steps = per_group // hb
    chunks = groups * steps
    scale = 1.0 / math.sqrt(width)

    def peer_h(k):
        return lax.rem(me_h + k, heads)

    def peer_s(k):
        return lax.rem(me_s + k, seqs)

    def row_copy(src, dst, send, recv, chunk, there, slot):
        part = pl.ds(chunk * hb, hb)
        return pltpu.make_async_remote_copy(
            src_ref=src.at[there, part], dst_ref=dst.at[slot, part],
            send_sem=send.at[chunk, there], recv_sem=recv.at[chunk, slot],
            device_id={"head": there}, device_id_type=MESH,
        )

    def kv_copy(there, slot):
        return pltpu.make_async_remote_copy(
            src_ref=kv_all.at[me_s], dst_ref=kv_all.at[slot],
            send_sem=kv_send.at[there], recv_sem=kv_recv.at[slot],
            device_id={"seq": there}, device_id_type=MESH,
        )

    partner = me_s + 1 - 2 * lax.rem(me_s, 2)

    def pass_copy(slot):
        return pltpu.make_async_remote_copy(
            src_ref=kv_all.at[slot], dst_ref=kv_all.at[slot],
            send_sem=pass_send.at[slot], recv_sem=kv_recv.at[slot],
            device_id={"seq": partner}, device_id_type=MESH,
        )

    def term_copy(group, kind, there, slot):
        send, recv = ((old_send, old_recv), (new_send, new_recv))[kind]
        return pltpu.make_async_remote_copy(
            src_ref=term_out.at[group, kind, there], dst_ref=term_in.at[group, kind, slot],
            send_sem=send.at[group, there], recv_sem=recv.at[group, slot],
            device_id={"seq": there}, device_id_type=MESH,
        )

    for kind, ref in enumerate((ko_ref, vo_ref, kn_ref, vn_ref)):
        kv_all[me_s, kind] = ref[...]

    barrier = pltpu.get_barrier_semaphore()
    for k in range(1, heads):
        pl.semaphore_signal(barrier, inc=1, device_id={"head": peer_h(k)}, device_id_type=MESH)
    for k in range(1, seqs):
        pl.semaphore_signal(barrier, inc=1, device_id={"seq": peer_s(k)}, device_id_type=MESH)
    pl.semaphore_wait(barrier, heads + seqs - 2)

    @pl.loop(1, seqs // 2)
    def _(k):
        kv_copy(peer_s(2 * k), me_s).start()

    kv_copy(partner, me_s).start()

    @pl.loop(0, chunks)
    def _(chunk):
        for k in range(1, heads):
            row_copy(q_ref, q_all, q_send, q_recv, chunk, peer_h(k), me_h).start()
            row_copy(do_ref, do_all, do_send, do_recv, chunk, peer_h(k), me_h).start()

    q_all[me_h] = q_ref[me_h]
    do_all[me_h] = do_ref[me_h]

    @pl.loop(1, seqs // 2)
    def _(k):
        slot = peer_s(2 * k)
        kv_copy(slot, slot).wait_recv()
        pass_copy(slot).start()

    @pl.loop(0, seqs // 2)
    def _(k):
        slot = lax.rem(partner + 2 * k, seqs)
        kv_copy(slot, slot).wait_recv()

    base = lax.rem(off_ref[0] + me_s * tokens, total)
    old_rows = total - me_s * tokens

    def slot_of(row):
        slot = row + base
        return jnp.where(slot >= total, slot - total, slot)

    @pl.loop(0, seqs - me_s)
    def _(block):
        row = block * tokens + lax.broadcasted_iota(jnp.int32, (tokens, total), 0)
        slot = lax.broadcasted_iota(jnp.int32, (tokens, total), 1)
        pick = jnp.where(slot_of(row) == slot, 1.0, 0.0).astype(jnp.bfloat16)
        for kind in range(2):
            stored = kv_all[:, kind].reshape(total, groups * width)
            line[kind, pl.ds(block * tokens, tokens)] = dot(pick, stored, NN).astype(jnp.bfloat16)

    @pl.loop(0, me_s + 1)
    def _(block):
        for kind in range(2):
            line[kind, pl.ds((seqs - me_s + block) * tokens, tokens)] = kv_all[block, 2 + kind]

    for group in range(groups):
        left = group * width
        window = win_ref[group]
        place = lax.broadcasted_iota(jnp.int32, (span, tokens), 0) - total
        token = lax.broadcasted_iota(jnp.int32, (span, tokens), 1)
        bias[...] = jnp.where((place <= token) & (place > token - window), 0.0, -jnp.inf)
        keys_t[...] = line[0, :, left : left + width].T
        sums[...] = jnp.zeros_like(sums)

        @pl.loop(0, steps)
        def _(step):
            chunk = group * steps + step
            first = chunk * hb
            for k in range(1, heads):
                row_copy(q_ref, q_all, q_send, q_recv, chunk, peer_h(k), peer_h(k)).wait_recv()
                row_copy(do_ref, do_all, do_send, do_recv, chunk, peer_h(k), peer_h(k)).wait_recv()
            q = jnp.concatenate([q_all[:, first + h].reshape(tokens, width) for h in range(hb)], 0)
            do = jnp.concatenate([do_all[:, first + h].reshape(tokens, width) for h in range(hb)], 0)
            keys = line[0, :, left : left + width]
            values = line[1, :, left : left + width]
            scores = dot(keys, q, NT) + jnp.concatenate([bias[...]] * hb, 1)
            top = jnp.max(scores, axis=0, keepdims=True)
            grown = jnp.exp2((scores - top) * (scale * math.log2(math.e)))
            inverse = 1.0 / jnp.sum(grown, axis=0, keepdims=True)
            weight_grad = dot(values, do, NT)
            delta = jnp.sum(grown * weight_grad, axis=0, keepdims=True) * inverse
            weights = grown * inverse
            dscore = (weights * (weight_grad - delta)).astype(jnp.bfloat16)
            dqt = dot(keys_t[...], dscore, NN) * scale
            for h in range(hb):
                piece = dqt[:, h * tokens : (h + 1) * tokens].T.astype(jnp.bfloat16)
                dq_out[:, first + h] = piece.reshape(heads, rows, width)
            for k in range(1, heads):
                row_copy(dq_out, dq_in, dq_send, dq_recv, chunk, peer_h(k), me_h).start()
            sums[:, :width] += dot(dscore, q, NN)
            sums[:, width:] += dot(weights.astype(jnp.bfloat16), do, NN)

        terms[:, :width] = (sums[:, :width] * scale).astype(jnp.bfloat16)
        terms[:, width:] = sums[:, width:].astype(jnp.bfloat16)

        @pl.loop(0, seqs)
        def _(k):
            there = peer_s(k)
            row = lax.broadcasted_iota(jnp.int32, (tokens, total), 1)
            slot = there * tokens + lax.broadcasted_iota(jnp.int32, (tokens, total), 0)
            chosen = (slot_of(row) == slot) & (row < old_rows)
            pick = jnp.where(chosen, 1.0, 0.0).astype(jnp.bfloat16)
            term_out[group, 0, there] = dot(pick, terms[:total], NN).astype(jnp.bfloat16)

            @pl.when(there <= me_s)
            def _():
                term_out[group, 1, there] = terms[pl.ds((seqs - me_s + there) * tokens, tokens)]

            @pl.when(k > 0)
            def _():
                term_copy(group, 0, there, me_s).start()

                @pl.when(there < me_s)
                def _():
                    term_copy(group, 1, there, me_s).start()

    for k in range(heads):
        there = peer_h(k)
        place = pl.ds(there * groups * per_group, groups * per_group)
        if k == 0:
            dq_ref[place] = dq_out[there]
            continue

        @pl.loop(0, chunks)
        def _(chunk):
            row_copy(dq_out, dq_in, dq_send, dq_recv, chunk, there, there).wait_recv()

        dq_ref[place] = dq_in[there]

    for group in range(groups):
        for kind in range(2):
            grad_ref[group, kind] = term_out[group, kind, me_s].astype(jnp.float32)

        @pl.loop(1, seqs)
        def _(k):
            there = peer_s(k)
            term_copy(group, 0, there, there).wait_recv()
            grad_ref[group, 0] += term_in[group, 0, there].astype(jnp.float32)

            @pl.when(there > me_s)
            def _():
                term_copy(group, 1, there, there).wait_recv()
                grad_ref[group, 1] += term_in[group, 1, there].astype(jnp.float32)

    kv_copy(partner, me_s).wait_send()

    @pl.loop(1, seqs // 2)
    def _(k):
        kv_copy(peer_s(2 * k), me_s).wait_send()
        pass_copy(peer_s(2 * k)).wait_send()

    @pl.loop(0, chunks)
    def _(chunk):
        for k in range(1, heads):
            row_copy(q_ref, q_all, q_send, q_recv, chunk, peer_h(k), me_h).wait_send()
            row_copy(do_ref, do_all, do_send, do_recv, chunk, peer_h(k), me_h).wait_send()
            row_copy(dq_out, dq_in, dq_send, dq_recv, chunk, peer_h(k), me_h).wait_send()

    @pl.loop(1, seqs)
    def _(k):
        there = peer_s(k)
        for group in range(groups):
            term_copy(group, 0, there, me_s).wait_send()

            @pl.when(there < me_s)
            def _():
                term_copy(group, 1, there, me_s).wait_send()


def kernel(
    heads, seqs, per_group, heads_at_once,
    win_ref, off_ref, q_ref, do_ref, ko_ref, vo_ref, kn_ref, vn_ref,
    dq_ref, grad_ref,
    wide, q_mine, do_mine, q_all, do_all, kv_all, line, keys_t, bias, sums, win_out, win_in, kv_ref,
    own_part, sib_out, sib_in, chip_sum, term_in, fold_in, fold_out, dq_out, dq_in,
    q_send, q_recv, do_send, do_recv, dq_send, dq_recv, win_sems,
    far_send, far_recv, plane_send, sib_send, kv_recv,
    part_send, part_recv, term_send, term_recv, fold_recv, back_send,
):
    hb = heads_at_once
    half = heads // 2
    chips = seqs // 2
    me_h, me_s = lax.axis_index("head"), lax.axis_index("seq")
    chip, side = me_s // 2, lax.rem(me_s, 2)
    sibling = chip * 2 + 1 - side
    pair, place = me_h // half, lax.rem(me_h, half)
    far_h = lax.rem(me_h + half, heads)
    rows, all_heads, width = q_ref.shape
    mine = all_heads // heads
    groups = mine // per_group
    tokens = rows * heads
    run = rows * half
    total = tokens * seqs
    span = total + run
    steps = per_group // hb
    scale = 1.0 / math.sqrt(width)
    first_token = me_s * tokens + pair * run
    narrow = jnp.bfloat16

    stages = [(0, 0)] + [(1, g) for g in range(groups)] + [(0, g) for g in range(1, groups)]
    stage_of = {key: at for at, key in enumerate(stages)}
    peers = []
    for dj in range(1, half):
        there = lax.rem(place + dj, half)
        peers.append((pair * half + there, there))

    def set_of(far, head):
        return lax.rem(head + half, heads) if far else head

    def chip_at(k):
        return lax.rem(chip + k, chips)

    def row_copy(src, dst, send, recv, stage, step, peer, from_slot, order):
        far, group = stages[stage]
        part = pl.ds(group * per_group + step * hb, hb)
        return pltpu.make_async_remote_copy(
            src_ref=src.at[from_slot, part], dst_ref=dst.at[far, place, part],
            send_sem=send.at[stage, step, peer[1]], recv_sem=recv.at[stage, step, order],
            device_id={"head": peer[0]}, device_id_type=MESH,
        )

    def q_copies(stage, step, peer, order):
        source = set_of(stages[stage][0], peer[0])
        return (
            row_copy(q_mine, q_all, q_send, q_recv, stage, step, peer, source, order),
            row_copy(do_mine, do_all, do_send, do_recv, stage, step, peer, source, order),
        )

    def dq_copy(stage, step, peer, order):
        far = stages[stage][0]
        return row_copy(dq_out.at[far], dq_in, dq_send, dq_recv, stage, step, peer, peer[1], order)

    def win_copy():
        return pltpu.make_async_remote_copy(
            src_ref=win_out, dst_ref=win_in, send_sem=win_sems.at[0], recv_sem=win_sems.at[1],
            device_id={"head": far_h}, device_id_type=MESH,
        )

    def far_copy(group, new):
        part = pl.ds(2 * new, 2)
        return pltpu.make_async_remote_copy(
            src_ref=kv_ref.at[group, part], dst_ref=kv_all.at[stage_of[1, group], me_s, part],
            send_sem=far_send.at[group, new], recv_sem=far_recv.at[group, new],
            device_id={"head": far_h}, device_id_type=MESH,
        )

    def plane_copy(stage, new, there):
        block = kv_all.at[stage, me_s, pl.ds(2 * new, 2)]
        return pltpu.make_async_remote_copy(
            src_ref=block, dst_ref=block,
            send_sem=plane_send.at[stage, new, there], recv_sem=kv_recv.at[stage, new, me_s],
            device_id={"seq": there * 2 + side}, device_id_type=MESH,
        )

    def sib_copy(stage, new, owner):
        block = kv_all.at[stage, owner, pl.ds(2 * new, 2)]
        return pltpu.make_async_remote_copy(
            src_ref=block, dst_ref=block,
            send_sem=sib_send.at[stage, new, owner // 2], recv_sem=kv_recv.at[stage, new, owner],
            device_id={"seq": sibling}, device_id_type=MESH,
        )

    def part_copy(stage, kind, there):
        return pltpu.make_async_remote_copy(
            src_ref=sib_out.at[stage, kind, there], dst_ref=sib_in.at[stage, kind, there],
            send_sem=part_send.at[stage, kind, there], recv_sem=part_recv.at[stage, kind, there],
            device_id={"seq": sibling}, device_id_type=MESH,
        )

    def term_copy(stage, kind, there, slot):
        far, group = stages[stage]
        dst, recv = (fold_in, fold_recv) if far else (term_in, term_recv)
        return pltpu.make_async_remote_copy(
            src_ref=chip_sum.at[stage, kind, there], dst_ref=dst.at[group, kind, slot],
            send_sem=term_send.at[stage, kind, there], recv_sem=recv.at[group, kind, slot],
            device_id={"seq": there * 2 + side}, device_id_type=MESH,
        )

    def back_copy(group, kind):
        return pltpu.make_async_remote_copy(
            src_ref=fold_out.at[group, kind], dst_ref=term_in.at[group, kind, chips],
            send_sem=back_send.at[group, kind], recv_sem=term_recv.at[group, kind, chips],
            device_id={"head": far_h}, device_id_type=MESH,
        )

    barrier = pltpu.get_barrier_semaphore()
    for there in [far_h] + [peer[0] for peer in peers]:
        pl.semaphore_signal(barrier, inc=1, device_id={"head": there}, device_id_type=MESH)
    for k in range(1, chips):
        pl.semaphore_signal(barrier, inc=1, device_id={"seq": chip_at(k) * 2 + side}, device_id_type=MESH)
    pl.semaphore_signal(barrier, inc=1, device_id={"seq": sibling}, device_id_type=MESH)

    for group in range(groups):
        win_out[group] = jnp.full(win_out.shape[1:], win_ref[group], jnp.int32)
        for kind, ref in enumerate((ko_ref, vo_ref, kn_ref, vn_ref)):
            kv_ref[group, kind] = ref[:, group]
        kv_all[stage_of[0, group], me_s] = kv_ref[group]

    pl.semaphore_wait(barrier, 1 + len(peers) + chips - 1 + 1)

    def share(stage, parts=(0, 1)):
        corner = chips - 1 - chip
        for new in parts:
            for there in (corner, chip + 1 - 2 * lax.rem(chip, 2), chip + 2 - 4 * (chip // 2)):
                @pl.when((there >= chip) | (new == 0))
                def _():
                    plane_copy(stage, new, there).start()

            sib_copy(stage, new, me_s).start()

    def relay(stage):
        for new in range(2):
            far_copy(stages[stage][1], new).wait_recv()
            share(stage, (new,))

    def service(stage):
        @pl.loop(1, chips)
        def _(k):
            there = chip_at(k)
            owner = there * 2 + side
            for new in range(2):
                @pl.when((there <= chip) | (new == 0))
                def _():
                    sib_copy(stage, new, owner).wait_recv()
                    sib_copy(stage, new, owner).start()

    def settle(stage):
        @pl.loop(0, chips)
        def _(there):
            owner = there * 2 + 1 - side
            for new in range(2):
                @pl.when((there <= chip) | (new == 0))
                def _():
                    sib_copy(stage, new, owner).wait_recv()

    def send_rows(stage, begin=0, end=steps):
        @pl.loop(begin, end)
        def _(step):
            for peer in peers:
                for copy in q_copies(stage, step, peer, place):
                    copy.start()

    for new in range(2):
        far_copy(0, new).start()
    share(0)
    for ref, out in ((q_ref, q_mine), (do_ref, do_mine)):
        wide[...] = ref[...].astype(jnp.float32).reshape(rows * all_heads, width)
        for head in range(all_heads):
            out[head // mine, head % mine] = wide[pl.ds(head, rows, stride=all_heads)].astype(narrow)
    send_rows(0)
    win_copy().start()
    for group in range(1, groups):
        for new in range(2):
            far_copy(group, new).start()
    for stage in range(1, len(stages)):
        send_rows(stage)

    for far in range(2):
        q_all[far, place] = q_mine[set_of(far, me_h)]
        do_all[far, place] = do_mine[set_of(far, me_h)]

    old_rows = pl.multiple_of(total - first_token, run)
    base = lax.rem(off_ref[0] + first_token, total)

    def build(stage):
        for kind in range(2):
            @pl.loop(0, seqs)
            def _(owner):
                sums[kind, pl.ds(owner * tokens, tokens)] = kv_all[stage, owner, kind].astype(jnp.float32)

            sums[kind, total : total + tokens] = sums[kind, :tokens]

            @pl.loop(0, (old_rows + tokens - 1) // tokens)
            def _(block):
                start = lax.rem(base + block * tokens, total)
                line[kind, pl.ds(pl.multiple_of(block * tokens, tokens), tokens)] = sums[
                    kind, pl.ds(start, tokens)
                ].astype(narrow)

            @pl.loop(0, me_s + 1)
            def _(block):
                line[kind, pl.ds(pl.multiple_of(old_rows + block * tokens, run), tokens)] = kv_all[stage, block, 2 + kind]

        far, group = stages[stage]
        window = (win_in if far else win_out)[group, :1]
        position = lax.broadcasted_iota(jnp.int32, bias.shape, 0) - total
        token = lax.rem(lax.broadcasted_iota(jnp.int32, bias.shape, 1), run)
        bias[...] = jnp.where((position <= token) & (position > token - window), 0.0, -jnp.inf)
        keys_t[...] = line[0, :span].T
        sums[...] = jnp.zeros_like(sums)

    def attend(stage, step):
        far, group = stages[stage]
        first = group * per_group + step * hb
        for peer in peers:
            for copy in q_copies(stage, step, peer, peer[1]):
                copy.wait_recv()
        q = jnp.concatenate([q_all[far, :, first + h].reshape(run, width) for h in range(hb)], 0)
        do = jnp.concatenate([do_all[far, :, first + h].reshape(run, width) for h in range(hb)], 0)
        scores = dot(line[0, :span], q, NT) + jnp.concatenate([bias[...]] * (hb * run // bias.shape[1]), 1)
        top = jnp.max(scores, axis=0, keepdims=True)
        grown = jnp.exp2((scores - top) * (scale * math.log2(math.e)))
        inverse = 1.0 / jnp.sum(grown, axis=0, keepdims=True)
        weight_grad = dot(line[1, :span], do, NT)
        delta = jnp.sum(grown * weight_grad, axis=0, keepdims=True) * inverse
        weights = grown * inverse
        dscore = (weights * (weight_grad - delta)).astype(narrow)
        dqt = dot(keys_t[...], dscore, NN) * scale
        for h in range(0, hb, 2):
            piece = dqt[:, h * run : (h + 2) * run].T.astype(narrow).reshape(2, half, rows, width)
            for k in range(2):
                dq_out[far, :, first + h + k] = piece[k]
        for peer in peers:
            dq_copy(stage, step, peer, place).start()
        sums[0, :span] += dot(dscore, q, NN)
        sums[1, :span] += dot(weights.astype(narrow), do, NN)

    def put(stage, kind, there, seq_side, load):
        k_part = load(0) * scale
        v_part = load(1)

        @pl.when(seq_side == side)
        def _():
            own_part[kind, there, :, :width] = k_part
            own_part[kind, there, :, width:] = v_part

        @pl.when(seq_side != side)
        def _():
            sib_out[stage, kind, there, :, :width] = k_part.astype(narrow)
            sib_out[stage, kind, there, :, width:] = v_part.astype(narrow)
            part_copy(stage, kind, there).start()

    def split(stage):
        @pl.loop(0, 2 * chip + 2)
        def _(block):
            part = pl.ds(pl.multiple_of(old_rows + block * tokens, run), tokens)
            put(stage, 1, block // 2, lax.rem(block, 2), lambda i: sums[i, part])

        @pl.loop(old_rows // run, total // run)
        def _(block):
            for kind in range(2):
                sums[kind, pl.ds(pl.multiple_of(block * run, run), run)] = jnp.zeros((run, width), jnp.float32)

        for kind in range(2):
            sums[kind, total : total + tokens] = sums[kind, :tokens]

        @pl.loop(0, seqs)
        def _(block):
            start = lax.rem(block * tokens + total - base, total)
            put(stage, 0, block // 2, lax.rem(block, 2), lambda i: sums[i, pl.ds(start, tokens)])

    def finish(stage):
        for kind in range(2):
            @pl.loop(0, chips)
            def _(k):
                there = chip_at(k + 1)

                @pl.when((there <= chip) | (kind == 0))
                def _():
                    part_copy(stage, kind, there).wait_recv()
                    both = own_part[kind, there] + sib_in[stage, kind, there].astype(jnp.float32)
                    chip_sum[stage, kind, there] = both.astype(narrow)

                    @pl.when(there != chip)
                    def _():
                        term_copy(stage, kind, there, chip).start()

    def gather(stage, kind):
        far, group = stages[stage]
        source = fold_in if far else term_in
        own_part[kind, 0] = chip_sum[stage, kind, chip].astype(jnp.float32)

        @pl.loop(1, chips)
        def _(k):
            there = chip_at(k)

            @pl.when((there >= chip) | (kind == 0))
            def _():
                term_copy(stage, kind, there, there).wait_recv()
                own_part[kind, 0] += source[group, kind, there].astype(jnp.float32)

    def fold(stage):
        group = stages[stage][1]
        for kind in range(2):
            gather(stage, kind)
            fold_out[group, kind] = own_part[kind, 0].astype(narrow)
            back_copy(group, kind).start()

    last = len(stages) - 1
    relay(1)
    service(0)
    settle(0)
    win_copy().wait_recv()
    for stage in range(last + 1):
        build(stage)

        @pl.loop(0, steps)
        def _(step):
            @pl.when(step == steps - 1)
            def _():
                if stage == 0:
                    for later in range(2, groups + 1):
                        relay(later)
                    for later in range(groups + 1, last + 1):
                        share(later)
                if stage > 0:
                    finish(stage - 1)
                if stage == last:
                    for group in range(groups - 1):
                        fold(stage_of[1, group])
                if stage < last:
                    service(stage + 1)

            attend(stage, step)

        split(stage)
        if stage < last:
            settle(stage + 1)

    finish(last)
    fold(stage_of[1, groups - 1])

    for far in range(2):
        dq_ref[pl.ds(set_of(far, me_h) * mine, mine)] = dq_out[far, place]
        for peer in peers:
            for group in range(groups):
                @pl.loop(0, steps)
                def _(step):
                    dq_copy(stage_of[far, group], step, peer, peer[1]).wait_recv()

            dq_ref[pl.ds(set_of(far, peer[0]) * mine, mine)] = dq_in[far, peer[1]]

    for group in range(groups):
        for kind in range(2):
            gather(stage_of[0, group], kind)
            back_copy(group, kind).wait_recv()
            own_part[kind, 0] += term_in[group, kind, chips].astype(jnp.float32)
            for part in range(2):
                grad_ref[kind * 2 + part, pl.ds(group, tokens, stride=groups)] = own_part[
                    kind, 0, :, part * width : (part + 1) * width
                ]

    win_copy().wait_send()
    for group in range(groups):
        for new in range(2):
            far_copy(group, new).wait_send()
        for kind in range(2):
            back_copy(group, kind).wait_send()
    for stage in range(last + 1):
        @pl.loop(0, steps)
        def _(step):
            for peer in peers:
                for copy in q_copies(stage, step, peer, place):
                    copy.wait_send()
                dq_copy(stage, step, peer, place).wait_send()

        for kind in range(2):
            sib_copy(stage, kind, me_s).wait_send()

            @pl.loop(1, chips)
            def _(k):
                there = chip_at(k)

                @pl.when((there >= chip) | (kind == 0))
                def _():
                    plane_copy(stage, kind, there).wait_send()

                @pl.when((there <= chip) | (kind == 0))
                def _():
                    sib_copy(stage, kind, there * 2 + side).wait_send()
                    term_copy(stage, kind, there, chip).wait_send()

            @pl.loop(0, chips)
            def _(there):
                @pl.when((there <= chip) | (kind == 0))
                def _():
                    part_copy(stage, kind, there).wait_send()


def plain_shards(query, key_new, value_new, key_old, value_old, offset, windows, grad_out):
    heads, seqs = lax.axis_size("head"), lax.axis_size("seq")
    rows, all_heads, width = query.shape
    tokens = rows * heads
    total = tokens * seqs
    groups = key_new.shape[1]
    span = total + tokens
    mine = all_heads // heads
    per_group = mine // groups
    hb = max(h for h in (1, 2, 4) if per_group % h == 0 and (h <= 1 or h * tokens * span <= 700_000))
    chunks = mine // hb

    def by_head(x):
        return x.transpose(1, 0, 2).reshape(heads, mine, rows, width)

    kv = [x.reshape(tokens, groups * width) for x in (key_old, value_old, key_new, value_new)]
    vmem = pl.BlockSpec(memory_space=pltpu.VMEM)
    smem = pl.BlockSpec(memory_space=pltpu.SMEM)
    narrow, wide = jnp.bfloat16, jnp.float32
    row_shape = (heads, mine, rows, width)
    row_sems = pltpu.SemaphoreType.DMA((chunks, heads))
    seq_sems = pltpu.SemaphoreType.DMA((seqs,))
    term_sems = pltpu.SemaphoreType.DMA((groups, seqs))
    term_shape = (groups, 2, seqs, tokens, 2 * width)
    dq, grads = pl.pallas_call(
        functools.partial(plain_kernel, heads, seqs, per_group, hb),
        in_specs=[smem, smem] + [vmem] * 6,
        out_specs=[vmem, vmem],
        out_shape=[
            jax.ShapeDtypeStruct((all_heads, rows, width), narrow),
            jax.ShapeDtypeStruct((groups, 2, tokens, 2 * width), wide),
        ],
        scratch_shapes=[
            pltpu.VMEM(row_shape, narrow),
            pltpu.VMEM(row_shape, narrow),
            pltpu.VMEM((seqs, 4, tokens, groups * width), narrow),
            pltpu.VMEM((2, span, groups * width), narrow),
            pltpu.VMEM((width, span), narrow),
            pltpu.VMEM((span, tokens), wide),
            pltpu.VMEM((span, 2 * width), wide),
            pltpu.VMEM((span, 2 * width), narrow),
            pltpu.VMEM(term_shape, narrow),
            pltpu.VMEM(term_shape, narrow),
            pltpu.VMEM(row_shape, narrow),
            pltpu.VMEM(row_shape, narrow),
            row_sems, row_sems, row_sems, row_sems, seq_sems, seq_sems, seq_sems,
            row_sems, row_sems, term_sems, term_sems, term_sems, term_sems,
        ],
        compiler_params=pltpu.CompilerParams(
            collective_id=0, has_side_effects=True, vmem_limit_bytes=62 * 2**20
        ),
    )(windows, offset, by_head(query), by_head(grad_out), *kv)
    grad_query = lax.optimization_barrier(dq.transpose(1, 0, 2)).astype(wide)
    grads = grads.reshape(groups, 2, tokens, 2, width).transpose(1, 3, 2, 0, 4)
    return (grad_query, grads[1, 0], grads[1, 1], grads[0, 0], grads[0, 1])


def shards(query, key_new, value_new, key_old, value_old, offset, windows, grad_out):
    heads, seqs = lax.axis_size("head"), lax.axis_size("seq")
    rows, all_heads, width = query.shape
    tokens = rows * heads
    total = tokens * seqs
    groups = key_new.shape[1]
    chips = seqs // 2
    half = heads // 2
    run = tokens // 2
    span = total + run
    padded = total + 2 * tokens
    mine = all_heads // heads
    per_group = mine // groups
    stages = 2 * groups
    budget = 60 * 2**20
    kept = total * width * (20 * stages + 8 * groups + 8) + 16 * padded * width + 20 * all_heads * rows * width
    fits = [h for h in (2, 4, 6) if per_group % h == 0 and 14 * h * run * span + kept < budget]
    if not fits or heads % 2 or seqs != 8:
        return plain_shards(query, key_new, value_new, key_old, value_old, offset, windows, grad_out)
    hb = max(fits)
    steps = per_group // hb

    vmem = pl.BlockSpec(memory_space=pltpu.VMEM)
    smem = pl.BlockSpec(memory_space=pltpu.SMEM)
    narrow, wide = jnp.bfloat16, jnp.float32
    row_shape = (heads, mine, rows, width)
    set_shape = (2, half, mine, rows, width)
    block = (tokens, 2 * width)
    dma = pltpu.SemaphoreType.DMA
    row_sems = dma((stages, steps, half))
    dq, grads = pl.pallas_call(
        functools.partial(kernel, heads, seqs, per_group, hb),
        in_specs=[smem, smem] + [vmem] * 6,
        out_specs=[vmem, vmem],
        out_shape=[
            jax.ShapeDtypeStruct((all_heads, rows, width), narrow),
            jax.ShapeDtypeStruct((4, tokens * groups, width), wide),
        ],
        scratch_shapes=[
            pltpu.VMEM((rows * all_heads, width), wide),
            pltpu.VMEM(row_shape, narrow),
            pltpu.VMEM(row_shape, narrow),
            pltpu.VMEM(set_shape, narrow),
            pltpu.VMEM(set_shape, narrow),
            pltpu.VMEM((stages, seqs, 4, tokens, width), narrow),
            pltpu.VMEM((2, padded, width), narrow),
            pltpu.VMEM((width, span), narrow),
            pltpu.VMEM((span, 2 * run), wide),
            pltpu.VMEM((2, padded, width), wide),
            pltpu.VMEM((groups, 8, 2 * run), jnp.int32),
            pltpu.VMEM((groups, 8, 2 * run), jnp.int32),
            pltpu.VMEM((groups, 4, tokens, width), narrow),
            pltpu.VMEM((2, chips) + block, wide),
            pltpu.VMEM((stages, 2, chips) + block, narrow),
            pltpu.VMEM((stages, 2, chips) + block, narrow),
            pltpu.VMEM((stages, 2, chips) + block, narrow),
            pltpu.VMEM((groups, 2, chips + 1) + block, narrow),
            pltpu.VMEM((groups, 2, chips) + block, narrow),
            pltpu.VMEM((groups, 2) + block, narrow),
            pltpu.VMEM(set_shape, narrow),
            pltpu.VMEM(set_shape, narrow),
            row_sems, row_sems, row_sems, row_sems, row_sems, row_sems, dma((2,)),
            dma((groups, 2)), dma((groups, 2)), dma((stages, 2, chips)), dma((stages, 2, chips)), dma((stages, 2, seqs)),
            dma((stages, 2, chips)), dma((stages, 2, chips)), dma((stages, 2, chips)),
            dma((groups, 2, chips + 1)), dma((groups, 2, chips)), dma((groups, 2)),
        ],
        compiler_params=pltpu.CompilerParams(
            collective_id=0, has_side_effects=True, vmem_limit_bytes=62 * 2**20
        ),
    )(windows, offset, query, grad_out, key_old, value_old, key_new, value_new)
    grad_query = lax.optimization_barrier(dq.transpose(1, 0, 2)).astype(wide)
    grads = grads.reshape(4, tokens, groups, width)
    return (grad_query, grads[2], grads[3], grads[0], grads[1])


def solution(mesh):
    tokens = P(("seq", "head"), None, None)
    slots = P("seq", "head", None)
    return jax.shard_map(
        shards,
        mesh=mesh,
        in_specs=(tokens, slots, slots, slots, slots, P(), P("head"), tokens),
        out_specs=(tokens, slots, slots, slots, slots),
        check_vma=False,
    )
```
